512 devices in a mesh: layer: 64 (over x, z), row: 8 (over y, core).
Axes of the slice: x: 4, y: 4, z: 16, core: 2. Of those that a mesh axis runs over, the one named last changes fastest.
Arguments:
- coupling: bfloat16 [64, 1024, 1024], P('layer', 'row'), may hold values from -1 to 1, as said below
- band_off: int32 [64], P('layer'), may hold values from 0 to 32
- band_width: int32 [64], P('layer'), may hold values from 1 to 3
- incident: float32 [32, 1024], P(None, 'row'), may hold values from -6 to 6
- cotangent: float32 [32, 1024], P(None, 'row'), may hold values from -6 to 6
Outputs:
- transmitted: float32 [64, 32, 1024], P('layer', None, 'row')
- adjoint: float32 [64, 32, 1024], P('layer', None, 'row')
The draws below stay inside these ranges and needn't reach their ends.
Inputs may be any that keep to these rules, and one draw needn't show every extreme that they name: coupling is antisymmetric in its last two dimensions.
All inputs are finite; a program needn't handle non-finite values.
Results may differ from the reference program's by a relative error of at most 0.012.
The reference program's roundings to bfloat16 on the way count: a program that leaves them out, or rounds other values in their place, can miss the bound.
Values may be sent and summed in bfloat16 or wider, within the bound.
A program may use at most 64 MiB of HBM per device.

```python
import math
import jax
import jax.numpy as jnp
from jax import lax

M = 1024
BLOCK = 16
GROUP = 8
FIELDS = 32
LAYERS = 64


def draw_coupling(key, part):
    base = jax.random.normal(key, (LAYERS, M, M), jnp.float32)
    factor = 0.75 / math.sqrt(14.0 * BLOCK) / math.sqrt(2.0)
    return ((base - jnp.swapaxes(base, 1, 2)) * factor).astype(jnp.bfloat16)


def plant(drawn, stream_key, smallest, top_value):
    longest = drawn.shape.index(max(drawn.shape))
    spots = []
    for shift in (0, 1):
        where = [jax.random.randint(jax.random.fold_in(stream_key, axis), (), 0, length) for axis, length in enumerate(drawn.shape)]
        where[longest] = (where[longest] + shift) % drawn.shape[longest]
        spots.append(tuple(where))
    return drawn.at[spots[0]].set(smallest).at[spots[1]].set(top_value)


def steps_of(rng, extent, cuts, least, largest):
    level = 1.0
    for position, parts in cuts:
        draws = jax.random.uniform(jax.random.fold_in(jax.random.fold_in(rng, 6), position), (parts,), jnp.float32, least / len(cuts), largest / len(cuts))
        level = level * jnp.repeat(jnp.exp(draws), extent[position] // parts).reshape((-1,) + (1,) * (len(extent) - 1 - position))
    return level


def scatter_about(rng, dims, spread, most, split=(), kind=jnp.bfloat16):
    result = jax.random.normal(rng, dims, jnp.float32) * spread
    if len(split) > 0:
        result = steps_of(rng, dims, split, -0.22, 0.18) * result
    return jnp.clip(result, min=-most, max=most).astype(kind)


def setup_inputs(seed: int = 0) -> dict:
    streams_of = jax.random.split(jax.random.key(seed), 6)
    coupling = draw_coupling(jax.random.fold_in(streams_of[5], 71), 0)
    band_off = plant(jax.random.randint(streams_of[1], (LAYERS,), 0, M // (2 * BLOCK) + 1), jax.random.fold_in(streams_of[1], 1), 0, (M // (2 * BLOCK) + 1) - 1).astype(jnp.int32)
    band_width = plant(jax.random.randint(streams_of[2], (LAYERS,), 1, 4), jax.random.fold_in(streams_of[2], 1), 1, 3).astype(jnp.int32)
    incident = scatter_about(streams_of[3], (FIELDS, M), 1.0, 6.0, ((1, 8),), jnp.float32)
    cotangent = scatter_about(streams_of[4], (FIELDS, M), 1.0, 6.0, ((1, 8),), jnp.float32)
    return dict(coupling=coupling, band_off=band_off, band_width=band_width, incident=incident, cotangent=cotangent)


def band_mask(row_ids, col_ids, offset, half_width):
    diff = col_ids[None, :] // BLOCK - row_ids[:, None] // BLOCK
    return (jnp.abs(diff - offset) <= half_width) | (jnp.abs(diff + offset) <= half_width)


def layer_map(args):
    coupled, offset, half_width = args
    indices = jnp.arange(M, dtype=jnp.int32)
    banded = jnp.where(band_mask(indices, indices, offset, half_width), coupled, jnp.zeros_like(coupled))
    identity = jnp.eye(M, dtype=jnp.float32)
    section = (identity + banded.astype(jnp.float32) / 4.0).astype(jnp.bfloat16)
    for divisor in (3.0, 2.0, 1.0):
        section = (identity + jnp.dot(banded, section, preferred_element_type=jnp.float32) / divisor).astype(jnp.bfloat16)
    return section


def reference(coupling, band_off, band_width, incident, cotangent):
    layer_maps = lax.map(layer_map, (coupling, band_off, band_width))

    def forward(field_now, one_map):
        nxt = jnp.dot(field_now, one_map.astype(jnp.float32).T, precision=lax.Precision.HIGHEST)
        return nxt, nxt

    def backward(field_now, one_map):
        nxt = jnp.dot(field_now, one_map.astype(jnp.float32), precision=lax.Precision.HIGHEST)
        return nxt, nxt

    _, forward_all = lax.scan(forward, incident, layer_maps)
    _, backward_all = lax.scan(backward, cotangent, layer_maps, reverse=True)
    transmitted = jnp.repeat(forward_all[GROUP - 1::GROUP], GROUP, axis=0)
    adjoint = jnp.repeat(backward_all[0::GROUP], GROUP, axis=0)
    return transmitted, adjoint
```

```python
import jax
import jax.numpy as jnp
from jax import lax
from jax.experimental import pallas as pl
from jax.experimental.pallas import tpu as pltpu
from jax.sharding import PartitionSpec as P

MESH = pl.DeviceIdType.MESH
BLOCK = 16
GROUP = 8
GROUPS = 8
ROWS = 8
PANELS = 4
ORDERS = 1024
TILE = 128
TILES = ORDERS // TILE
PANEL = ORDERS // PANELS
CHUNK = TILE + 16
FIELDS = 32
LINE = 2 * GROUP
REACH = 6
STRIP = 256
f32 = jnp.float32
bf16 = jnp.bfloat16


def role_layer(group, kind):
    odd = group % 2
    return LINE * (group // 2) + jnp.where(kind == 0, GROUP - 1 + odd, (LINE - 1) * odd)


def kernel(off_ref, width_ref, coupling_ref, incident_ref, cotangent_ref, sent_ref, back_ref,
           local, packs, flipped, banded, carry, even, odd, weights, field_in, chain_in, chain_out, spread, landed,
           load_sem, pack_send, pack_recv, ring_send, ring_recv, field_send, field_recv,
           chain_send, chain_recv, spread_send, spread_recv):
    layer = lax.axis_index("layer")
    row = lax.axis_index("row")
    y = row // 2
    core = row % 2
    group = layer // GROUP
    inner = layer % GROUP
    lead = (role_layer(group, 0), role_layer(group, 1))
    is_role = [(core == 0) & (layer == lead[0]), (core == 0) & (layer == lead[1])]
    role = is_role[0] | is_role[1]
    kind = jnp.where(layer == lead[1], 1, 0)
    place = jnp.where(kind == 0, group, GROUPS - 1 - group)
    first = place == 0
    final = place == GROUPS - 1
    follow = role_layer(jnp.where(kind == 0, jnp.minimum(group + 1, GROUPS - 1), jnp.maximum(group - 1, 0)), kind)
    precede = role_layer(jnp.where(kind == 0, jnp.maximum(group - 1, 0), jnp.minimum(group + 1, GROUPS - 1)), kind)
    start_layers = (role_layer(0, 0), role_layer(GROUPS - 1, 1))
    at_start = (layer == start_layers[0]) | (layer == start_layers[1])

    load = pltpu.make_async_copy(coupling_ref.at[0], local, load_sem.at[0])
    load.start()
    own_field = field_in.at[row]
    field_loads = [
        pltpu.make_async_copy(source, own_field, load_sem.at[1]) for source in (incident_ref, cotangent_ref)
    ]
    for which in range(2):
        @pl.when(layer == start_layers[which])
        def _(which=which):
            field_loads[which].start()

    barrier = pltpu.get_barrier_semaphore()

    def greet(to_layer, to_row):
        pl.semaphore_signal(barrier, inc=1, device_id={"layer": to_layer, "row": to_row}, device_id_type=MESH)

    for which in range(2):
        @pl.when(jnp.logical_not(is_role[which]))
        def _(which=which):
            greet(lead[which], 2 * y)

    @pl.when(role)
    def _():
        for i in range(GROUP):
            for c in range(2):
                @pl.when((i != inner) | (c != core))
                def _(i=i, c=c):
                    greet(GROUP * group + i, 2 * y + c)
        for step in range(1, PANELS):
            greet(layer, 2 * ((y + step) % PANELS))

        @pl.when(jnp.logical_not(first))
        def _():
            for p in range(PANELS):
                greet(precede, 2 * p)

        @pl.when(first)
        def _():
            for step in range(1, PANELS):
                greet(layer, 2 * ((y + step) % PANELS) + 1)

    load.wait()
    offset = off_ref[0].astype(f32)
    half_width = width_ref[0].astype(f32)
    block_row = lax.broadcasted_iota(jnp.int32, (TILE, TILE), 0) // BLOCK
    block_col = lax.broadcasted_iota(jnp.int32, (TILE, TILE), 1) // BLOCK
    relative = (block_col - block_row).astype(f32)
    ahead = (GROUP * row).astype(f32)
    folded = jnp.zeros((TILE, TILE), f32)
    for s in range(TILES):
        d = relative + (8.0 * s - ahead)
        upper = (d >= 0) & (jnp.abs(d - offset) <= half_width)
        folded = folded + jnp.where(upper, local[:, TILE * s:TILE * s + TILE].astype(f32), 0.0)
    packs[inner, row, 0:TILE, :] = folded.astype(bf16)
    tail = lax.broadcasted_iota(jnp.int32, (16, TILE), 0)
    packs[inner, row, TILE:CHUNK, :] = jnp.where(tail < 8, offset, half_width).astype(bf16)
    for which in range(2):
        @pl.when(layer == start_layers[which])
        def _(which=which):
            field_loads[which].wait()

    expected = jnp.where(role, 2 * GROUP + PANELS - 1 + jnp.where(final, 0, PANELS), 2)
    expected = expected + jnp.where(at_start & (core == 1), PANELS - 1, 0)
    pl.semaphore_wait(barrier, expected)

    def pack_copy(which, i, r, to_layer):
        return pltpu.make_async_remote_copy(
            src_ref=packs.at[i, r], dst_ref=packs.at[i, r],
            send_sem=pack_send.at[which], recv_sem=pack_recv.at[i, r % 2],
            device_id={"layer": to_layer, "row": 2 * y}, device_id_type=MESH)

    for which in range(2):
        @pl.when(jnp.logical_not(is_role[which]))
        def _(which=which):
            pack_copy(which, inner, row, lead[which]).start()

    def field_copy(step):
        return pltpu.make_async_remote_copy(
            src_ref=field_in.at[row], dst_ref=field_in.at[row],
            send_sem=field_send.at[step], recv_sem=field_recv.at[row],
            device_id={"layer": layer, "row": 2 * ((y + step) % PANELS)}, device_id_type=MESH)

    @pl.when(at_start)
    def _():
        for step in range(PANELS):
            @pl.when((core == 1) | (step != 0))
            def _(step=step):
                field_copy(step).start()

    def spread_copy(i, c, which):
        return pltpu.make_async_remote_copy(
            src_ref=spread.at[c], dst_ref=landed.at[which],
            send_sem=spread_send.at[i, c], recv_sem=spread_recv.at[which],
            device_id={"layer": GROUP * group + i, "row": 2 * y + c}, device_id_type=MESH)

    @pl.when(role)
    def _():
        forward_order = (kind == 1) != first
        sign = jnp.where(forward_order, 1.0, -1.0).astype(f32)

        def nth(k):
            return jnp.where(forward_order, k, GROUP - 1 - k)

        def ring_copy(i, step):
            other = 2 * ((y + step) % PANELS)
            return pltpu.make_async_remote_copy(
                src_ref=packs.at[i, pl.ds(2 * y, 2)], dst_ref=packs.at[i, pl.ds(2 * y, 2)],
                send_sem=ring_send.at[i, step], recv_sem=ring_recv.at[i, y],
                device_id={"layer": layer, "row": other}, device_id_type=MESH)

        def ring_arrival(i, step):
            source = (y + step) % PANELS
            return pltpu.make_async_remote_copy(
                src_ref=packs.at[i, pl.ds(2 * source, 2)], dst_ref=packs.at[i, pl.ds(2 * source, 2)],
                send_sem=ring_send.at[i, step], recv_sem=ring_recv.at[i, source],
                device_id={"layer": layer, "row": 2 * source}, device_id_type=MESH)

        def pass_round(k):
            i = nth(k)

            @pl.when(i != inner)
            def _():
                pack_copy(0, i, 2 * y, lead[0]).wait_recv()
            pack_copy(0, i, 2 * y + 1, lead[0]).wait_recv()
            for step in range(1, PANELS):
                ring_copy(i, step).start()

        pass_round(0)
        pass_round(1)

        @pl.when(first)
        def _():
            for r in range(ROWS):
                @pl.when(r != row)
                def _(r=r):
                    pltpu.make_async_remote_copy(
                        src_ref=field_in.at[r], dst_ref=field_in.at[r],
                        send_sem=field_send.at[0], recv_sem=field_recv.at[r],
                        device_id={"layer": layer, "row": (row + 1) % ROWS}, device_id_type=MESH).wait_recv()
                tall = jnp.concatenate([field_in[r], jnp.zeros((TILE - FIELDS, TILE), f32)], axis=0)
                carry[TILE * r:TILE * r + TILE, 0:TILE] = tall.T
            carry[:, TILE:PANEL] = jnp.zeros((ORDERS, PANEL - TILE), f32)

        @pl.when(jnp.logical_not(first))
        def _():
            rows_at = lax.broadcasted_iota(jnp.int32, (ORDERS, PANEL), 0)
            cols_at = lax.broadcasted_iota(jnp.int32, (ORDERS, PANEL), 1)
            carry[...] = jnp.where(rows_at == cols_at + PANEL * y, 1.0, 0.0).astype(f32)

        even[...] = carry[...].astype(bf16)
        blank = jnp.zeros((TILE, TILE), bf16)

        @pl.loop(0, GROUP)
        def _(k):
            @pl.when(k + 2 < GROUP)
            def _():
                pass_round(k + 2)
            i = nth(k)
            for step in range(1, PANELS):
                ring_arrival(i, step).wait_recv()
            off = packs[i, 0, TILE:TILE + 1, :].astype(f32)
            wide = packs[i, 0, TILE + 8:TILE + 9, :].astype(f32)

            def upper_mask(apart):
                d = relative + 8.0 * apart
                return jnp.where((d >= 0) & (jnp.abs(d - off) <= wide), 1.0, 0.0).astype(bf16)

            def lower_mask(apart):
                d = relative - 8.0 * apart
                return jnp.where((d < 0) & (jnp.abs(d + off) <= wide), -1.0, 0.0).astype(bf16)

            uppers = [upper_mask(apart) for apart in range(REACH)]
            lowers = [lower_mask(apart) for apart in range(REACH)]
            for t in range(TILES):
                flipped[:, TILE * t:TILE * t + TILE] = packs[i, t, 0:TILE, :].T
            for t in range(TILES):
                for s in range(TILES):
                    there = slice(TILE * s, TILE * s + TILE)
                    if abs(s - t) >= REACH:
                        value = blank
                    elif s > t:
                        value = packs[i, t, 0:TILE, :] * uppers[s - t]
                    elif s < t:
                        value = flipped[:, there] * lowers[t - s]
                    else:
                        value = packs[i, t, 0:TILE, :] * uppers[0] + flipped[:, there] * lowers[0]
                    banded[TILE * t:TILE * t + TILE, there] = value
            for divisor, source, target in ((4.0, even, odd), (3.0, odd, even), (2.0, even, odd), (1.0, odd, None)):
                for strip in range(0, ORDERS, STRIP):
                    here = slice(strip, strip + STRIP)
                    moved = jnp.dot(banded[here, :], source[...], preferred_element_type=f32)
                    total = carry[here, :] + moved * (sign / divisor)
                    if target is None:
                        carry[here, :] = total
                        even[here, :] = total.astype(bf16)
                    else:
                        target[here, :] = total.astype(bf16)

        @pl.when(first)
        def _():
            mine = carry[pl.ds(pl.multiple_of(PANEL * y, PANEL), PANEL), 0:TILE]
            chain_out[...] = mine.T[0:FIELDS, :]

        @pl.when(jnp.logical_not(first))
        def _():
            for strip in range(0, ORDERS, STRIP):
                here = slice(strip, strip + STRIP)
                value = carry[here, :]
                high = value.astype(bf16)
                weights[here, 0:PANEL] = high
                weights[here, PANEL:2 * PANEL] = (value - high.astype(f32)).astype(bf16)
            for p in range(PANELS):
                pltpu.make_async_remote_copy(
                    src_ref=chain_out, dst_ref=chain_in.at[p],
                    send_sem=chain_send.at[0], recv_sem=chain_recv.at[p],
                    device_id={"layer": precede, "row": 2 * p}, device_id_type=MESH).wait_recv()
            summed = jnp.zeros((2 * FIELDS, 2 * PANEL), f32)
            for p in range(PANELS):
                value = chain_in[p]
                high = value.astype(bf16)
                low = (value - high.astype(f32)).astype(bf16)
                both = jnp.concatenate([high, low], axis=0)
                summed = summed + jnp.dot(both, weights[PANEL * p:PANEL * p + PANEL, :], preferred_element_type=f32)
            chain_out[...] = (summed[0:FIELDS, 0:PANEL] + summed[FIELDS:, 0:PANEL]
                              + summed[0:FIELDS, PANEL:] + summed[FIELDS:, PANEL:])

        def chain_copy(p):
            return pltpu.make_async_remote_copy(
                src_ref=chain_out, dst_ref=chain_in.at[y],
                send_sem=chain_send.at[p], recv_sem=chain_recv.at[y],
                device_id={"layer": follow, "row": 2 * p}, device_id_type=MESH)

        @pl.when(jnp.logical_not(final))
        def _():
            for p in range(PANELS):
                chain_copy(p).start()

        for c in range(2):
            spread[c] = chain_out[:, TILE * c:TILE * c + TILE].astype(bf16)
        landed[kind] = spread[0]
        for i in range(GROUP):
            for c in range(2):
                @pl.when((i != inner) | (c != core))
                def _(i=i, c=c):
                    spread_copy(i, c, kind).start()

        for i in range(GROUP):
            for step in range(1, PANELS):
                ring_copy(i, step).wait_send()

        @pl.when(jnp.logical_not(final))
        def _():
            for p in range(PANELS):
                chain_copy(p).wait_send()
        for i in range(GROUP):
            for c in range(2):
                @pl.when((i != inner) | (c != core))
                def _(i=i, c=c):
                    spread_copy(i, c, kind).wait_send()

    for which in range(2):
        @pl.when(jnp.logical_not(is_role[which]))
        def _(which=which):
            pack_copy(which, inner, row, lead[which]).wait_send()

    @pl.when(at_start)
    def _():
        for step in range(PANELS):
            @pl.when((core == 1) | (step != 0))
            def _(step=step):
                field_copy(step).wait_send()

    for which, out in ((0, sent_ref), (1, back_ref)):
        @pl.when(jnp.logical_not(is_role[which]))
        def _(which=which):
            pltpu.make_async_remote_copy(
                src_ref=spread.at[0], dst_ref=landed.at[which],
                send_sem=spread_send.at[0, 0], recv_sem=spread_recv.at[which],
                device_id={"layer": lead[which], "row": 2 * y}, device_id_type=MESH).wait_recv()
        out[...] = landed[which]


def on_device(coupling, band_off, band_width, incident, cotangent):
    smem = pl.BlockSpec(memory_space=pltpu.SMEM)
    vmem = pl.BlockSpec(memory_space=pltpu.VMEM)
    away = pl.BlockSpec(memory_space=pl.ANY)
    dma = pltpu.SemaphoreType.DMA
    share = jax.ShapeDtypeStruct((FIELDS, TILE), bf16)
    sent, back = pl.pallas_call(
        kernel,
        out_shape=(share, share),
        in_specs=[smem, smem, away, away, away],
        out_specs=(vmem, vmem),
        scratch_shapes=[
            pltpu.VMEM((TILE, ORDERS), bf16),
            pltpu.VMEM((GROUP, ROWS, CHUNK, TILE), bf16),
            pltpu.VMEM((TILE, ORDERS), bf16),
            pltpu.VMEM((ORDERS, ORDERS), bf16),
            pltpu.VMEM((ORDERS, PANEL), f32),
            pltpu.VMEM((ORDERS, PANEL), bf16),
            pltpu.VMEM((ORDERS, PANEL), bf16),
            pltpu.VMEM((ORDERS, 2 * PANEL), bf16),
            pltpu.VMEM((ROWS, FIELDS, TILE), f32),
            pltpu.VMEM((PANELS, FIELDS, PANEL), f32),
            pltpu.VMEM((FIELDS, PANEL), f32),
            pltpu.VMEM((2, FIELDS, TILE), bf16),
            pltpu.VMEM((2, FIELDS, TILE), bf16),
            dma((2,)), dma((2,)), dma((GROUP, 2)), dma((GROUP, PANELS)), dma((GROUP, PANELS)),
            dma((PANELS,)), dma((ROWS,)), dma((PANELS,)), dma((PANELS,)), dma((GROUP, 2)), dma((2,)),
        ],
        compiler_params=pltpu.CompilerParams(collective_id=0, has_side_effects=True),
        name="cascade",
    )(band_off, band_width, coupling, incident, cotangent)
    return sent.astype(f32)[None], back.astype(f32)[None]


def solution(mesh):
    in_specs = (P("layer", "row", None), P("layer"), P("layer"), P(None, "row"), P(None, "row"))
    out_specs = (P("layer", None, "row"), P("layer", None, "row"))
    return jax.shard_map(
        on_device, mesh=mesh, in_specs=in_specs, out_specs=out_specs, check_vma=False
    )
```

```python
import jax
import jax.numpy as jnp
from jax import lax
from jax.experimental import pallas as pl
from jax.experimental.pallas import tpu as pltpu
from jax.sharding import PartitionSpec as P

MESH = pl.DeviceIdType.MESH
BLOCK = 16
GROUP = 8
GROUPS = 8
ROWS = 8
PANELS = 4
ORDERS = 1024
TILE = 128
TILES = ORDERS // TILE
PANEL = ORDERS // PANELS
FIELDS = 32
LINE = 2 * GROUP
WIDEST = 3
WINDOW = 256
LEAD = 576
TRAIL = 640
PADDED = LEAD + ORDERS + TRAIL
SPAN = WINDOW // BLOCK
f32 = jnp.float32
bf16 = jnp.bfloat16


def role_layer(group, kind):
    return LINE * (group // 2) + jnp.where(kind == 0, GROUP - 1, 0)


def kernel(off_ref, width_ref, coupling_ref, incident_ref, cotangent_ref, sent_ref, back_ref,
           scalars, local, mine, note, packs, notes, offsets, plain, banded, carry, high, low, even, odd,
           field_in, chain_in, chain_out, landed,
           load_sem, pack_send, pack_recv, note_send, note_recv, note_load, ring_send, ring_recv,
           field_send, field_recv, chain_send, chain_recv, spread_send, spread_recv):
    layer = lax.axis_index("layer")
    row = lax.axis_index("row")
    y = row // 2
    core = row % 2
    place_z = layer % LINE
    pair = layer // LINE
    own_group = layer // GROUP
    inner = layer % GROUP
    parity = own_group % 2
    targets = ((role_layer(own_group, 0), 2 * y + parity), (role_layer(own_group, 1), 2 * y + parity))
    is_target = [(layer == targets[w][0]) & (row == targets[w][1]) for w in range(2)]
    inside = is_target[0] | is_target[1]
    role = (place_z == 0) | (place_z == GROUP - 1)
    kind = jnp.where(place_z == 0, 1, 0)
    group = 2 * pair + core
    place = jnp.where(kind == 0, group, GROUPS - 1 - group)
    first = place == 0
    final = place == GROUPS - 1
    ahead = jnp.where(kind == 0, jnp.minimum(group + 1, GROUPS - 1), jnp.maximum(group - 1, 0))
    behind = jnp.where(kind == 0, jnp.maximum(group - 1, 0), jnp.minimum(group + 1, GROUPS - 1))
    start_layers = (role_layer(0, 0), role_layer(GROUPS - 1, 1))
    at_start = (layer == start_layers[0]) | (layer == start_layers[1])
    start_core = jnp.where(layer == start_layers[0], 0, 1)
    up = (y + 1) % PANELS
    down = (y + PANELS - 1) % PANELS

    load = pltpu.make_async_copy(coupling_ref.at[0], local, load_sem.at[0])
    load.start()
    off_load = pltpu.make_async_copy(off_ref, scalars.at[0], load_sem.at[2])
    width_load = pltpu.make_async_copy(width_ref, scalars.at[1], load_sem.at[3])
    off_load.start()
    width_load.start()
    field_loads = [
        pltpu.make_async_copy(source, field_in.at[row], load_sem.at[1]) for source in (incident_ref, cotangent_ref)
    ]
    for which in range(2):
        @pl.when(layer == start_layers[which])
        def _(which=which):
            field_loads[which].start()

    barrier = pltpu.get_barrier_semaphore()

    def greet(to_layer, to_row):
        pl.semaphore_signal(barrier, inc=1, device_id={"layer": to_layer, "row": to_row}, device_id_type=MESH)

    for which in range(2):
        @pl.when(jnp.logical_not(is_target[which]))
        def _(which=which):
            greet(*targets[which])

    @pl.when(role)
    def _():
        for i in range(GROUP):
            for c in range(2):
                @pl.when((GROUP * group + i != layer) | (c != core))
                def _(i=i, c=c):
                    greet(GROUP * group + i, 2 * y + c)
        greet(layer, 2 * up + core)
        greet(layer, 2 * down + core)

        @pl.when(jnp.logical_not(first))
        def _():
            for p in range(PANELS):
                greet(role_layer(behind, kind), 2 * p + behind % 2)

        @pl.when(first)
        def _():
            for step in range(1, ROWS):
                greet(layer, (row + step) % ROWS)

        for buffer in (high, low, even, odd):
            buffer[0:LEAD // BLOCK] = jnp.zeros((LEAD // BLOCK, BLOCK, PANEL), bf16)
            buffer[(LEAD + ORDERS) // BLOCK:PADDED // BLOCK] = jnp.zeros((TRAIL // BLOCK, BLOCK, PANEL), bf16)
        plain[0:LEAD // BLOCK] = jnp.zeros((LEAD // BLOCK, BLOCK, TILE), bf16)
        plain[(LEAD + ORDERS) // BLOCK:PADDED // BLOCK] = jnp.zeros((TRAIL // BLOCK, BLOCK, TILE), bf16)

    off_load.wait()
    width_load.wait()
    offset = scalars[0, 0]
    half_width = scalars[1, 0]
    note[...] = jnp.full((8, TILE), offset, jnp.int32)
    load.wait()
    here_row = lax.broadcasted_iota(jnp.int32, (TILE, TILE), 0) + TILE * row
    here_col = lax.broadcasted_iota(jnp.int32, (TILE, TILE), 1)
    folded = jnp.zeros((TILE, TILE), f32)
    for s in range(TILES):
        there = here_col + TILE * s
        apart = there // BLOCK - here_row // BLOCK
        upper = (there > here_row) & (jnp.abs(apart - offset) <= half_width)
        folded = folded + jnp.where(upper, local[:, TILE * s:TILE * s + TILE].astype(f32), 0.0)
    mine[...] = folded.astype(bf16)

    @pl.when(inside)
    def _():
        packs[inner, row] = mine[...]

        @pl.when(core == 0)
        def _():
            notes[inner] = note[...]

    for which in range(2):
        @pl.when(layer == start_layers[which])
        def _(which=which):
            field_loads[which].wait()

    expected = jnp.where(inside, 1, 2)
    expected = expected + jnp.where(role, 2 * GROUP + 2 - jnp.where(inside, 1, 0) + jnp.where(final, 0, PANELS), 0)
    expected = expected + jnp.where(at_start, PANELS - jnp.where(core == start_core, 1, 0), 0)
    pl.semaphore_wait(barrier, expected)

    def pack_copy(which):
        return pltpu.make_async_remote_copy(
            src_ref=mine, dst_ref=packs.at[inner, row],
            send_sem=pack_send.at[which], recv_sem=pack_recv.at[inner, core],
            device_id={"layer": targets[which][0], "row": targets[which][1]}, device_id_type=MESH)

    def note_copy(which):
        return pltpu.make_async_remote_copy(
            src_ref=note, dst_ref=notes.at[inner],
            send_sem=note_send.at[which], recv_sem=note_recv.at[inner],
            device_id={"layer": targets[which][0], "row": targets[which][1]}, device_id_type=MESH)

    for which in range(2):
        @pl.when(jnp.logical_not(is_target[which]))
        def _(which=which):
            pack_copy(which).start()

            @pl.when(core == 0)
            def _():
                note_copy(which).start()

    def field_copy(step):
        return pltpu.make_async_remote_copy(
            src_ref=field_in.at[row], dst_ref=field_in.at[row],
            send_sem=field_send.at[step], recv_sem=field_recv.at[row],
            device_id={"layer": layer, "row": 2 * ((y + step) % PANELS) + start_core}, device_id_type=MESH)

    @pl.when(at_start)
    def _():
        for step in range(PANELS):
            @pl.when((core != start_core) | (step != 0))
            def _(step=step):
                field_copy(step).start()

    def spread_copy(i, c):
        return pltpu.make_async_remote_copy(
            src_ref=chain_out.at[:, pl.ds(TILE * c, TILE)], dst_ref=landed.at[kind],
            send_sem=spread_send.at[i, c], recv_sem=spread_recv.at[kind],
            device_id={"layer": GROUP * group + i, "row": 2 * y + c}, device_id_type=MESH)

    @pl.when(role)
    def _():
        forward_order = (kind == 1) != first
        sign = jnp.where(forward_order, 1.0, -1.0).astype(f32)

        def nth(k):
            return jnp.where(forward_order, k, GROUP - 1 - k)

        def local_pack(i, c):
            return (GROUP * group + i == layer) & (c == core)

        def wait_pack(i, c):
            @pl.when(jnp.logical_not(local_pack(i, c)))
            def _():
                pltpu.make_async_remote_copy(
                    src_ref=mine, dst_ref=packs.at[i, 2 * y + c],
                    send_sem=pack_send.at[0], recv_sem=pack_recv.at[i, c],
                    device_id={"layer": layer, "row": 2 * up + core}, device_id_type=MESH).wait_recv()

        def pair_copy(i, toward, slot):
            return pltpu.make_async_remote_copy(
                src_ref=packs.at[i, pl.ds(2 * y, 2)], dst_ref=packs.at[i, pl.ds(2 * y, 2)],
                send_sem=ring_send.at[i, slot], recv_sem=ring_recv.at[i, slot],
                device_id={"layer": layer, "row": 2 * toward + core}, device_id_type=MESH)

        def pair_wait(i, source, slot):
            pltpu.make_async_remote_copy(
                src_ref=packs.at[i, pl.ds(2 * source, 2)], dst_ref=packs.at[i, pl.ds(2 * source, 2)],
                send_sem=ring_send.at[i, slot], recv_sem=ring_recv.at[i, slot],
                device_id={"layer": layer, "row": 2 * source + core}, device_id_type=MESH).wait_recv()

        def half_copy(i, r, toward, slot):
            return pltpu.make_async_remote_copy(
                src_ref=packs.at[i, r], dst_ref=packs.at[i, r],
                send_sem=ring_send.at[i, slot], recv_sem=ring_recv.at[i, slot],
                device_id={"layer": layer, "row": 2 * toward + core}, device_id_type=MESH)

        across = (y + 2) % PANELS

        def send_round(k):
            i = nth(k)
            wait_pack(i, 0)
            wait_pack(i, 1)
            pair_copy(i, up, 0).start()
            pair_copy(i, down, 1).start()

        def relay_round(k):
            i = nth(k)
            pair_wait(i, down, 0)
            half_copy(i, 2 * down, up, 2).start()
            pair_wait(i, up, 1)
            half_copy(i, 2 * up + 1, down, 3).start()

        def finish_round(k):
            i = nth(k)
            half_copy(i, 2 * across, up, 2).wait_recv()
            half_copy(i, 2 * across + 1, down, 3).wait_recv()

        def note_fetch(i):
            return pltpu.make_async_copy(notes.at[i], offsets.at[i], note_load.at[i])

        send_round(0)
        send_round(1)

        @pl.when(first)
        def _():
            for r in range(ROWS):
                @pl.when(r != row)
                def _(r=r):
                    pltpu.make_async_remote_copy(
                        src_ref=field_in.at[r], dst_ref=field_in.at[r],
                        send_sem=field_send.at[0], recv_sem=field_recv.at[r],
                        device_id={"layer": layer, "row": (row + 1) % ROWS}, device_id_type=MESH).wait_recv()
                tall = jnp.concatenate([field_in[r], jnp.zeros((TILE - FIELDS, TILE), f32)], axis=0)
                carry[TILE * r:TILE * r + TILE, 0:TILE] = tall.T
            carry[:, TILE:PANEL] = jnp.zeros((ORDERS, PANEL - TILE), f32)

        @pl.when(jnp.logical_not(first))
        def _():
            rows_at = lax.broadcasted_iota(jnp.int32, (ORDERS, PANEL), 0)
            cols_at = lax.broadcasted_iota(jnp.int32, (ORDERS, PANEL), 1)
            carry[...] = jnp.where(rows_at == cols_at + PANEL * y, 1.0, 0.0).astype(f32)

        def blocks_of(t):
            return slice((LEAD + TILE * t) // BLOCK, (LEAD + TILE * t + TILE) // BLOCK)

        def split(t, value):
            here = blocks_of(t)
            top = value.astype(bf16)
            high[here] = top.reshape(TILE // BLOCK, BLOCK, PANEL)
            low[here] = (value - top.astype(f32)).astype(bf16).reshape(TILE // BLOCK, BLOCK, PANEL)

        for t in range(TILES):
            split(t, carry[TILE * t:TILE * t + TILE, :])

        slot = lax.broadcasted_iota(jnp.int32, (TILE, WINDOW), 1) // BLOCK
        step = lax.broadcasted_iota(jnp.int32, (TILE, WINDOW), 0) // BLOCK
        near = jnp.abs(slot - step - WIDEST) <= WIDEST
        upper_mask = jnp.where(near, sign, 0.0).astype(bf16)
        lower_mask = jnp.where(near, -sign, 0.0).astype(bf16)

        relay_round(0)

        @pl.loop(0, GROUP)
        def _(k):
            @pl.when(k + 2 < GROUP)
            def _():
                send_round(k + 2)

            @pl.when(k + 1 < GROUP)
            def _():
                relay_round(k + 1)
            i = nth(k)

            @pl.when(jnp.logical_not(local_pack(i, 0)))
            def _():
                pltpu.make_async_remote_copy(
                    src_ref=note, dst_ref=notes.at[i],
                    send_sem=note_send.at[0], recv_sem=note_recv.at[i],
                    device_id={"layer": layer, "row": 2 * up + core}, device_id_type=MESH).wait_recv()
            note_fetch(i).start()
            finish_round(k)
            note_fetch(i).wait()
            off = offsets[i, 0, 0]
            turn = jnp.broadcast_to(WIDEST + 40 - notes[i, 0:1, :], (TILE, TILE))
            turns = [(turn & (1 << bit)) != 0 for bit in range(3)]

            def upper_at(t):
                return pl.ds((LEAD + TILE * t) // BLOCK - WIDEST + off, SPAN)

            def lower_at(t):
                return pl.ds((LEAD + TILE * t) // BLOCK - WIDEST - off, SPAN)

            for t in range(TILES):
                value = packs[i, t]
                plain[blocks_of(t)] = value.reshape(TILE // BLOCK, BLOCK, TILE)
                turned = value.astype(f32)
                for bit in range(3):
                    turned = jnp.where(turns[bit], pltpu.roll(turned, BLOCK << bit, 1), turned)
                turned = turned.astype(bf16)
                banded[t, :, 0:WINDOW] = jnp.concatenate([turned, turned], axis=1) * upper_mask
            for t in range(TILES):
                banded[t, :, WINDOW:2 * WINDOW] = plain[lower_at(t)].reshape(WINDOW, TILE).T * lower_mask

            def product(t, source):
                return (jnp.dot(banded[t, :, 0:WINDOW], source[upper_at(t)].reshape(WINDOW, PANEL), preferred_element_type=f32)
                        + jnp.dot(banded[t, :, WINDOW:2 * WINDOW], source[lower_at(t)].reshape(WINDOW, PANEL), preferred_element_type=f32))

            for order, source, target in ((1, high, even), (2, even, odd), (3, odd, even), (4, even, None)):
                for t in range(TILES):
                    here = slice(TILE * t, TILE * t + TILE)
                    term = product(t, source)
                    if order == 1:
                        term = term + product(t, low)
                    else:
                        term = term * (1.0 / order)
                    total = carry[here, :] + term
                    carry[here, :] = total
                    if target is None:
                        split(t, total)
                    else:
                        target[blocks_of(t)] = term.astype(bf16).reshape(TILE // BLOCK, BLOCK, PANEL)

        @pl.when(first)
        def _():
            part = carry[pl.ds(pl.multiple_of(PANEL * y, PANEL), PANEL), 0:TILE]
            chain_out[...] = part.T[0:FIELDS, :].astype(bf16)

        @pl.when(jnp.logical_not(first))
        def _():
            summed = jnp.zeros((FIELDS, PANEL), f32)
            for p in range(PANELS):
                pltpu.make_async_remote_copy(
                    src_ref=chain_out, dst_ref=chain_in.at[p],
                    send_sem=chain_send.at[0], recv_sem=chain_recv.at[p],
                    device_id={"layer": layer, "row": 2 * up + core}, device_id_type=MESH).wait_recv()
                summed = summed + jnp.dot(chain_in[p], high[(LEAD + PANEL * p) // BLOCK:(LEAD + PANEL * p + PANEL) // BLOCK].reshape(PANEL, PANEL),
                                          preferred_element_type=f32)
            chain_out[...] = summed.astype(bf16)

        def chain_copy(p):
            return pltpu.make_async_remote_copy(
                src_ref=chain_out, dst_ref=chain_in.at[y],
                send_sem=chain_send.at[p], recv_sem=chain_recv.at[y],
                device_id={"layer": role_layer(ahead, kind), "row": 2 * p + ahead % 2}, device_id_type=MESH)

        @pl.when(jnp.logical_not(final))
        def _():
            for p in range(PANELS):
                chain_copy(p).start()

        for i in range(GROUP):
            for c in range(2):
                @pl.when(jnp.logical_not(local_pack(i, c)))
                def _(i=i, c=c):
                    spread_copy(i, c).start()

        @pl.when(inside)
        def _():
            landed[kind] = jnp.where(core == 0, chain_out[:, 0:TILE], chain_out[:, TILE:PANEL])

        for i in range(GROUP):
            pair_copy(i, up, 0).wait_send()
            pair_copy(i, down, 1).wait_send()
            half_copy(i, 2 * down, up, 2).wait_send()
            half_copy(i, 2 * up + 1, down, 3).wait_send()

        @pl.when(jnp.logical_not(final))
        def _():
            for p in range(PANELS):
                chain_copy(p).wait_send()
        for i in range(GROUP):
            for c in range(2):
                @pl.when(jnp.logical_not(local_pack(i, c)))
                def _(i=i, c=c):
                    spread_copy(i, c).wait_send()

    for which in range(2):
        @pl.when(jnp.logical_not(is_target[which]))
        def _(which=which):
            pack_copy(which).wait_send()

            @pl.when(core == 0)
            def _():
                note_copy(which).wait_send()

    @pl.when(at_start)
    def _():
        for step in range(PANELS):
            @pl.when((core != start_core) | (step != 0))
            def _(step=step):
                field_copy(step).wait_send()

    for which, out in ((0, sent_ref), (1, back_ref)):
        @pl.when(jnp.logical_not(is_target[which]))
        def _(which=which):
            pltpu.make_async_remote_copy(
                src_ref=chain_out.at[:, pl.ds(0, TILE)], dst_ref=landed.at[which],
                send_sem=spread_send.at[0, 0], recv_sem=spread_recv.at[which],
                device_id={"layer": targets[which][0], "row": targets[which][1]}, device_id_type=MESH).wait_recv()
        out[...] = landed[which]


def on_device(coupling, band_off, band_width, incident, cotangent):
    vmem = pl.BlockSpec(memory_space=pltpu.VMEM)
    away = pl.BlockSpec(memory_space=pl.ANY)
    dma = pltpu.SemaphoreType.DMA
    share = jax.ShapeDtypeStruct((FIELDS, TILE), bf16)
    sent, back = pl.pallas_call(
        kernel,
        out_shape=(share, share),
        in_specs=[away] * 5,
        out_specs=(vmem, vmem),
        scratch_shapes=[
            pltpu.SMEM((2, 1), jnp.int32),
            pltpu.VMEM((TILE, ORDERS), bf16),
            pltpu.VMEM((TILE, TILE), bf16),
            pltpu.VMEM((8, TILE), jnp.int32),
            pltpu.VMEM((GROUP, ROWS, TILE, TILE), bf16),
            pltpu.VMEM((GROUP, 8, TILE), jnp.int32),
            pltpu.SMEM((GROUP, 8, TILE), jnp.int32),
            pltpu.VMEM((PADDED // BLOCK, BLOCK, TILE), bf16),
            pltpu.VMEM((TILES, TILE, 2 * WINDOW), bf16),
            pltpu.VMEM((ORDERS, PANEL), f32),
            pltpu.VMEM((PADDED // BLOCK, BLOCK, PANEL), bf16),
            pltpu.VMEM((PADDED // BLOCK, BLOCK, PANEL), bf16),
            pltpu.VMEM((PADDED // BLOCK, BLOCK, PANEL), bf16),
            pltpu.VMEM((PADDED // BLOCK, BLOCK, PANEL), bf16),
            pltpu.VMEM((ROWS, FIELDS, TILE), f32),
            pltpu.VMEM((PANELS, FIELDS, PANEL), bf16),
            pltpu.VMEM((FIELDS, PANEL), bf16),
            pltpu.VMEM((2, FIELDS, TILE), bf16),
            dma((4,)), dma((2,)), dma((GROUP, 2)), dma((2,)), dma((GROUP,)), dma((GROUP,)),
            dma((GROUP, 4)), dma((GROUP, 4)), dma((PANELS,)), dma((ROWS,)), dma((PANELS,)), dma((PANELS,)),
            dma((GROUP, 2)), dma((2,)),
        ],
        compiler_params=pltpu.CompilerParams(collective_id=0, has_side_effects=True),
        name="cascade",
    )(band_off, band_width, coupling, incident, cotangent)
    return sent.astype(f32)[None], back.astype(f32)[None]


def solution(mesh):
    in_specs = (P("layer", "row", None), P("layer"), P("layer"), P(None, "row"), P(None, "row"))
    out_specs = (P("layer", None, "row"), P("layer", None, "row"))
    return jax.shard_map(
        on_device, mesh=mesh, in_specs=in_specs, out_specs=out_specs, check_vma=False
    )
```

```python
import jax
import jax.numpy as jnp
from jax import lax
from jax.experimental import pallas as pl
from jax.experimental.pallas import tpu as pltpu
from jax.sharding import PartitionSpec as P

MESH = pl.DeviceIdType.MESH
BLOCK = 16
GROUP = 8
GROUPS = 8
ROWS = 8
PANELS = 4
ORDERS = 1024
TILE = 128
TILES = ORDERS // TILE
PANEL = ORDERS // PANELS
FIELDS = 32
LINE = 2 * GROUP
WIDEST = 3
WINDOW = 256
LEAD = 576
TRAIL = 640
PADDED = LEAD + ORDERS + TRAIL
SPAN = WINDOW // BLOCK
DIRECT = (0, 7)
FORWARD_Z = 7
f32 = jnp.float32
bf16 = jnp.bfloat16


def role_layer(group, kind):
    return LINE * (group // 2) + jnp.where(kind == 0, FORWARD_Z, 0)


def is_direct(i):
    found = i == DIRECT[0]
    for other in DIRECT[1:]:
        found = found | (i == other)
    return found


def kernel(off_ref, width_ref, coupling_ref, incident_ref, cotangent_ref, sent_ref, back_ref,
           scalars, local, mine, note, packs, notes, offsets, plain, flipped, banded, carry, high, low, even, odd,
           field_in, chain_in, chain_out, landed,
           load_sem, pack_send, pack_recv, note_send, note_recv, note_load, ring_send, ring_recv,
           field_send, field_recv, chain_send, chain_recv, spread_send, spread_recv):
    layer = lax.axis_index("layer")
    row = lax.axis_index("row")
    y = row // 2
    core = row % 2
    place_z = layer % LINE
    pair = layer // LINE
    own_group = layer // GROUP
    inner = layer % GROUP
    parity = own_group % 2
    targets = ((role_layer(own_group, 0), 2 * y + parity), (role_layer(own_group, 1), 2 * y + parity))
    is_target = [(layer == targets[w][0]) & (row == targets[w][1]) for w in range(2)]
    inside = is_target[0] | is_target[1]
    role = (place_z == 0) | (place_z == FORWARD_Z)
    kind = jnp.where(place_z == 0, 1, 0)
    group = 2 * pair + core
    place = jnp.where(kind == 0, group, GROUPS - 1 - group)
    first = place == 0
    final = place == GROUPS - 1
    ahead = jnp.where(kind == 0, jnp.minimum(group + 1, GROUPS - 1), jnp.maximum(group - 1, 0))
    behind = jnp.where(kind == 0, jnp.maximum(group - 1, 0), jnp.minimum(group + 1, GROUPS - 1))
    start_layers = (role_layer(0, 0), role_layer(GROUPS - 1, 1))
    at_start = (layer == start_layers[0]) | (layer == start_layers[1])
    start_core = jnp.where(layer == start_layers[0], 0, 1)
    up = (y + 1) % PANELS
    down = (y + PANELS - 1) % PANELS

    load = pltpu.make_async_copy(coupling_ref.at[0], local, load_sem.at[0])
    load.start()
    off_load = pltpu.make_async_copy(off_ref, scalars.at[0], load_sem.at[2])
    width_load = pltpu.make_async_copy(width_ref, scalars.at[1], load_sem.at[3])
    off_load.start()
    width_load.start()
    field_loads = [
        pltpu.make_async_copy(source, field_in.at[row], load_sem.at[1]) for source in (incident_ref, cotangent_ref)
    ]
    for which in range(2):
        @pl.when(layer == start_layers[which])
        def _(which=which):
            field_loads[which].start()

    barrier = pltpu.get_barrier_semaphore()

    def greet(to_layer, to_row):
        pl.semaphore_signal(barrier, inc=1, device_id={"layer": to_layer, "row": to_row}, device_id_type=MESH)

    for which in range(2):
        @pl.when(jnp.logical_not(is_target[which]))
        def _(which=which):
            greet(*targets[which])

    @pl.when(role)
    def _():
        for i in range(GROUP):
            for r in range(ROWS) if i in DIRECT else (2 * y, 2 * y + 1):
                @pl.when((GROUP * group + i != layer) | (r != row))
                def _(i=i, r=r):
                    greet(GROUP * group + i, r)
        greet(layer, 2 * up + core)
        greet(layer, 2 * down + core)

        @pl.when(jnp.logical_not(first))
        def _():
            for p in range(PANELS):
                greet(role_layer(behind, kind), 2 * p + behind % 2)

        @pl.when(first)
        def _():
            for step in range(1, ROWS):
                greet(layer, (row + step) % ROWS)

        for buffer in (high, low, even, odd):
            buffer[0:LEAD // BLOCK] = jnp.zeros((LEAD // BLOCK, BLOCK, PANEL), bf16)
            buffer[(LEAD + ORDERS) // BLOCK:PADDED // BLOCK] = jnp.zeros((TRAIL // BLOCK, BLOCK, PANEL), bf16)
        plain[0:LEAD // BLOCK] = jnp.zeros((LEAD // BLOCK, BLOCK, TILE), bf16)
        plain[(LEAD + ORDERS) // BLOCK:PADDED // BLOCK] = jnp.zeros((TRAIL // BLOCK, BLOCK, TILE), bf16)

    off_load.wait()
    width_load.wait()
    offset = scalars[0, 0]
    half_width = scalars[1, 0]
    note[...] = jnp.full((8, TILE), offset, jnp.int32)
    load.wait()
    here_row = lax.broadcasted_iota(jnp.int32, (TILE, TILE), 0) + TILE * row
    here_col = lax.broadcasted_iota(jnp.int32, (TILE, TILE), 1)
    folded = jnp.zeros((TILE, TILE), f32)
    for s in range(TILES):
        there = here_col + TILE * s
        apart = there // BLOCK - here_row // BLOCK
        upper = (there > here_row) & (jnp.abs(apart - offset) <= half_width)
        folded = folded + jnp.where(upper, local[:, TILE * s:TILE * s + TILE].astype(f32), 0.0)
    turn = jnp.broadcast_to(WIDEST + 40 - note[0:1, :], (TILE, TILE))
    for bit in range(3):
        folded = jnp.where((turn & (1 << bit)) != 0, pltpu.roll(folded, BLOCK << bit, 1), folded)
    mine[...] = folded.astype(bf16)

    @pl.when(inside)
    def _():
        packs[inner, row] = mine[...]

        @pl.when(core == 0)
        def _():
            notes[inner] = note[...]

    for which in range(2):
        @pl.when(layer == start_layers[which])
        def _(which=which):
            field_loads[which].wait()

    direct = is_direct(inner)
    expected = jnp.where(direct, 2 * PANELS, 2) - jnp.where(inside, 1, 0)
    expected = expected + jnp.where(role, 2 * GROUP + 2 - jnp.where(inside, 1, 0) + jnp.where(final, 0, PANELS), 0)
    expected = expected + jnp.where(at_start, PANELS - jnp.where(core == start_core, 1, 0), 0)
    pl.semaphore_wait(barrier, expected)

    def pack_copy(which, step):
        return pltpu.make_async_remote_copy(
            src_ref=mine, dst_ref=packs.at[inner, row],
            send_sem=pack_send.at[which, step], recv_sem=pack_recv.at[inner, row],
            device_id={"layer": targets[which][0], "row": 2 * ((y + step) % PANELS) + parity}, device_id_type=MESH)

    def note_copy(which):
        return pltpu.make_async_remote_copy(
            src_ref=note, dst_ref=notes.at[inner],
            send_sem=note_send.at[which], recv_sem=note_recv.at[inner],
            device_id={"layer": targets[which][0], "row": targets[which][1]}, device_id_type=MESH)

    for which in range(2):
        @pl.when(jnp.logical_not(is_target[which]))
        def _(which=which):
            pack_copy(which, 0).start()

            @pl.when(core == 0)
            def _():
                note_copy(which).start()

    @pl.when(direct)
    def _():
        for which in range(2):
            for step in range(1, PANELS):
                pack_copy(which, step).start()

    def field_copy(step):
        return pltpu.make_async_remote_copy(
            src_ref=field_in.at[row], dst_ref=field_in.at[row],
            send_sem=field_send.at[step], recv_sem=field_recv.at[row],
            device_id={"layer": layer, "row": 2 * ((y + step) % PANELS) + start_core}, device_id_type=MESH)

    @pl.when(at_start)
    def _():
        for step in range(PANELS):
            @pl.when((core != start_core) | (step != 0))
            def _(step=step):
                field_copy(step).start()

    def spread_copy(i, c):
        return pltpu.make_async_remote_copy(
            src_ref=chain_out.at[:, pl.ds(TILE * c, TILE)], dst_ref=landed.at[kind],
            send_sem=spread_send.at[i, c], recv_sem=spread_recv.at[kind],
            device_id={"layer": GROUP * group + i, "row": 2 * y + c}, device_id_type=MESH)

    @pl.when(role)
    def _():
        forward_order = (kind == 1) != first
        sign = jnp.where(forward_order, 1.0, -1.0).astype(f32)

        def nth(k):
            return jnp.where(forward_order, k, GROUP - 1 - k)

        def local_pack(i, c):
            return (GROUP * group + i == layer) & (c == core)

        def wait_pack(i, r):
            @pl.when((GROUP * group + i != layer) | (r != row))
            def _():
                pltpu.make_async_remote_copy(
                    src_ref=mine, dst_ref=packs.at[i, r],
                    send_sem=pack_send.at[0, 0], recv_sem=pack_recv.at[i, r],
                    device_id={"layer": layer, "row": 2 * up + core}, device_id_type=MESH).wait_recv()

        def pair_copy(i, toward, slot):
            return pltpu.make_async_remote_copy(
                src_ref=packs.at[i, pl.ds(2 * y, 2)], dst_ref=packs.at[i, pl.ds(2 * y, 2)],
                send_sem=ring_send.at[i, slot], recv_sem=ring_recv.at[i, slot],
                device_id={"layer": layer, "row": 2 * toward + core}, device_id_type=MESH)

        def pair_wait(i, source, slot):
            pltpu.make_async_remote_copy(
                src_ref=packs.at[i, pl.ds(2 * source, 2)], dst_ref=packs.at[i, pl.ds(2 * source, 2)],
                send_sem=ring_send.at[i, slot], recv_sem=ring_recv.at[i, slot],
                device_id={"layer": layer, "row": 2 * source + core}, device_id_type=MESH).wait_recv()

        def half_copy(i, r, toward, slot):
            return pltpu.make_async_remote_copy(
                src_ref=packs.at[i, r], dst_ref=packs.at[i, r],
                send_sem=ring_send.at[i, slot], recv_sem=ring_recv.at[i, slot],
                device_id={"layer": layer, "row": 2 * toward + core}, device_id_type=MESH)

        across = (y + 2) % PANELS

        def send_round(k):
            i = nth(k)

            @pl.when(jnp.logical_not(is_direct(i)))
            def _():
                wait_pack(i, 2 * y)
                wait_pack(i, 2 * y + 1)
                pair_copy(i, up, 0).start()
                pair_copy(i, down, 1).start()

        def relay_round(k):
            i = nth(k)

            @pl.when(jnp.logical_not(is_direct(i)))
            def _():
                pair_wait(i, down, 0)
                half_copy(i, 2 * down, up, 2).start()
                pair_wait(i, up, 1)
                half_copy(i, 2 * up + 1, down, 3).start()

        def finish_round(k):
            i = nth(k)

            @pl.when(jnp.logical_not(is_direct(i)))
            def _():
                half_copy(i, 2 * across, up, 2).wait_recv()
                half_copy(i, 2 * across + 1, down, 3).wait_recv()

            @pl.when(is_direct(i))
            def _():
                for r in range(ROWS):
                    wait_pack(i, r)

        def note_fetch(i):
            return pltpu.make_async_copy(notes.at[i], offsets.at[i], note_load.at[i])

        def note_round(k):
            i = nth(k)

            @pl.when(jnp.logical_not(local_pack(i, 0)))
            def _():
                pltpu.make_async_remote_copy(
                    src_ref=note, dst_ref=notes.at[i],
                    send_sem=note_send.at[0], recv_sem=note_recv.at[i],
                    device_id={"layer": layer, "row": 2 * up + core}, device_id_type=MESH).wait_recv()
            note_fetch(i).start()

        send_round(0)
        send_round(1)

        @pl.when(first)
        def _():
            for r in range(ROWS):
                @pl.when(r != row)
                def _(r=r):
                    pltpu.make_async_remote_copy(
                        src_ref=field_in.at[r], dst_ref=field_in.at[r],
                        send_sem=field_send.at[0], recv_sem=field_recv.at[r],
                        device_id={"layer": layer, "row": (row + 1) % ROWS}, device_id_type=MESH).wait_recv()
                tall = jnp.concatenate([field_in[r], jnp.zeros((TILE - FIELDS, TILE), f32)], axis=0)
                carry[TILE * r:TILE * r + TILE, 0:TILE] = tall.T
            carry[:, TILE:PANEL] = jnp.zeros((ORDERS, PANEL - TILE), f32)

        @pl.when(jnp.logical_not(first))
        def _():
            rows_at = lax.broadcasted_iota(jnp.int32, (ORDERS, PANEL), 0)
            cols_at = lax.broadcasted_iota(jnp.int32, (ORDERS, PANEL), 1)
            carry[...] = jnp.where(rows_at == cols_at + PANEL * y, 1.0, 0.0).astype(f32)

        def blocks_of(t):
            return slice((LEAD + TILE * t) // BLOCK, (LEAD + TILE * t + TILE) // BLOCK)

        def split(t, value):
            here = blocks_of(t)
            top = value.astype(bf16)
            high[here] = top.reshape(TILE // BLOCK, BLOCK, PANEL)
            low[here] = (value - top.astype(f32)).astype(bf16).reshape(TILE // BLOCK, BLOCK, PANEL)

        for t in range(TILES):
            split(t, carry[TILE * t:TILE * t + TILE, :])

        slot = lax.broadcasted_iota(jnp.int32, (TILE, WINDOW), 1) // BLOCK
        step = lax.broadcasted_iota(jnp.int32, (TILE, WINDOW), 0) // BLOCK
        near = jnp.abs(slot - step - WIDEST) <= WIDEST
        upper_mask = jnp.where(near, sign, 0.0).astype(bf16)
        lower_mask = jnp.where(near, -sign, 0.0).astype(bf16)

        note_round(0)
        relay_round(0)

        @pl.loop(0, GROUP)
        def _(k):
            @pl.when(k + 2 < GROUP)
            def _():
                send_round(k + 2)

            @pl.when(k + 1 < GROUP)
            def _():
                relay_round(k + 1)

            @pl.when(k + 1 < GROUP)
            def _():
                note_round(k + 1)
            i = nth(k)
            finish_round(k)
            note_fetch(i).wait()
            off = offsets[i, 0, 0]
            turn = (WIDEST + 40 - off) % 8

            def upper_at(t):
                return pl.ds((LEAD + TILE * t) // BLOCK - WIDEST + off, SPAN)

            def lower_at(t):
                return pl.ds((LEAD + TILE * t) // BLOCK - WIDEST - off, SPAN)

            for t in range(TILES):
                value = packs[i, t]
                plain[blocks_of(t)] = value.reshape(TILE // BLOCK, BLOCK, TILE)
                banded[t, :, 0:WINDOW] = jnp.concatenate([value, value], axis=1) * upper_mask
            for t in range(TILES):
                tall = plain[lower_at(t)].reshape(WINDOW, TILE).T.reshape(TILE // BLOCK, BLOCK, WINDOW)
                flipped[t, 0:TILE // BLOCK] = tall
                flipped[t, TILE // BLOCK:2 * TILE // BLOCK] = tall
            for t in range(TILES):
                tall = flipped[t, pl.ds(turn, TILE // BLOCK)].reshape(TILE, WINDOW)
                banded[t, :, WINDOW:2 * WINDOW] = tall * lower_mask

            def product(t, source):
                both = jnp.concatenate([source[upper_at(t)].reshape(WINDOW, PANEL),
                                        source[lower_at(t)].reshape(WINDOW, PANEL)], axis=0)
                return jnp.dot(banded[t], both, preferred_element_type=f32)

            for order, source, target in ((1, high, even), (2, even, odd), (3, odd, even), (4, even, None)):
                for t in range(TILES):
                    here = slice(TILE * t, TILE * t + TILE)
                    term = product(t, source)
                    if order == 1:
                        term = term + product(t, low)
                    else:
                        term = term * (1.0 / order)
                    total = carry[here, :] + term
                    carry[here, :] = total
                    if target is None:
                        split(t, total)
                    else:
                        target[blocks_of(t)] = term.astype(bf16).reshape(TILE // BLOCK, BLOCK, PANEL)

        @pl.when(first)
        def _():
            part = carry[pl.ds(pl.multiple_of(PANEL * y, PANEL), PANEL), 0:TILE]
            chain_out[...] = part.T[0:FIELDS, :].astype(bf16)

        @pl.when(jnp.logical_not(first))
        def _():
            summed = jnp.zeros((FIELDS, PANEL), f32)
            for p in range(PANELS):
                pltpu.make_async_remote_copy(
                    src_ref=chain_out, dst_ref=chain_in.at[p],
                    send_sem=chain_send.at[0], recv_sem=chain_recv.at[p],
                    device_id={"layer": layer, "row": 2 * up + core}, device_id_type=MESH).wait_recv()
                summed = summed + jnp.dot(chain_in[p], high[(LEAD + PANEL * p) // BLOCK:(LEAD + PANEL * p + PANEL) // BLOCK].reshape(PANEL, PANEL),
                                          preferred_element_type=f32)
            chain_out[...] = summed.astype(bf16)

        def chain_copy(p):
            return pltpu.make_async_remote_copy(
                src_ref=chain_out, dst_ref=chain_in.at[y],
                send_sem=chain_send.at[p], recv_sem=chain_recv.at[y],
                device_id={"layer": role_layer(ahead, kind), "row": 2 * p + ahead % 2}, device_id_type=MESH)

        @pl.when(jnp.logical_not(final))
        def _():
            for p in range(PANELS):
                chain_copy(p).start()

        for i in range(GROUP):
            for c in range(2):
                @pl.when(jnp.logical_not(local_pack(i, c)))
                def _(i=i, c=c):
                    spread_copy(i, c).start()

        @pl.when(inside)
        def _():
            landed[kind] = jnp.where(core == 0, chain_out[:, 0:TILE], chain_out[:, TILE:PANEL])

        for i in [j for j in range(GROUP) if j not in DIRECT]:
            pair_copy(i, up, 0).wait_send()
            pair_copy(i, down, 1).wait_send()
            half_copy(i, 2 * down, up, 2).wait_send()
            half_copy(i, 2 * up + 1, down, 3).wait_send()

        @pl.when(jnp.logical_not(final))
        def _():
            for p in range(PANELS):
                chain_copy(p).wait_send()
        for i in range(GROUP):
            for c in range(2):
                @pl.when(jnp.logical_not(local_pack(i, c)))
                def _(i=i, c=c):
                    spread_copy(i, c).wait_send()

    for which in range(2):
        @pl.when(jnp.logical_not(is_target[which]))
        def _(which=which):
            pack_copy(which, 0).wait_send()

            @pl.when(core == 0)
            def _():
                note_copy(which).wait_send()

    @pl.when(direct)
    def _():
        for which in range(2):
            for step in range(1, PANELS):
                pack_copy(which, step).wait_send()

    @pl.when(at_start)
    def _():
        for step in range(PANELS):
            @pl.when((core != start_core) | (step != 0))
            def _(step=step):
                field_copy(step).wait_send()

    for which, out in ((0, sent_ref), (1, back_ref)):
        @pl.when(jnp.logical_not(is_target[which]))
        def _(which=which):
            pltpu.make_async_remote_copy(
                src_ref=chain_out.at[:, pl.ds(0, TILE)], dst_ref=landed.at[which],
                send_sem=spread_send.at[0, 0], recv_sem=spread_recv.at[which],
                device_id={"layer": targets[which][0], "row": targets[which][1]}, device_id_type=MESH).wait_recv()
        out[...] = landed[which]


def on_device(coupling, band_off, band_width, incident, cotangent):
    vmem = pl.BlockSpec(memory_space=pltpu.VMEM)
    away = pl.BlockSpec(memory_space=pl.ANY)
    dma = pltpu.SemaphoreType.DMA
    share = jax.ShapeDtypeStruct((FIELDS, TILE), bf16)
    sent, back = pl.pallas_call(
        kernel,
        out_shape=(share, share),
        in_specs=[away] * 5,
        out_specs=(vmem, vmem),
        scratch_shapes=[
            pltpu.SMEM((2, 1), jnp.int32),
            pltpu.VMEM((TILE, ORDERS), bf16),
            pltpu.VMEM((TILE, TILE), bf16),
            pltpu.VMEM((8, TILE), jnp.int32),
            pltpu.VMEM((GROUP, ROWS, TILE, TILE), bf16),
            pltpu.VMEM((GROUP, 8, TILE), jnp.int32),
            pltpu.SMEM((GROUP, 8, TILE), jnp.int32),
            pltpu.VMEM((PADDED // BLOCK, BLOCK, TILE), bf16),
            pltpu.VMEM((TILES, 2 * TILE // BLOCK, BLOCK, WINDOW), bf16),
            pltpu.VMEM((TILES, TILE, 2 * WINDOW), bf16),
            pltpu.VMEM((ORDERS, PANEL), f32),
            pltpu.VMEM((PADDED // BLOCK, BLOCK, PANEL), bf16),
            pltpu.VMEM((PADDED // BLOCK, BLOCK, PANEL), bf16),
            pltpu.VMEM((PADDED // BLOCK, BLOCK, PANEL), bf16),
            pltpu.VMEM((PADDED // BLOCK, BLOCK, PANEL), bf16),
            pltpu.VMEM((ROWS, FIELDS, TILE), f32),
            pltpu.VMEM((PANELS, FIELDS, PANEL), bf16),
            pltpu.VMEM((FIELDS, PANEL), bf16),
            pltpu.VMEM((2, FIELDS, TILE), bf16),
            dma((4,)), dma((2, PANELS)), dma((GROUP, ROWS)), dma((2,)), dma((GROUP,)), dma((GROUP,)),
            dma((GROUP, 4)), dma((GROUP, 4)), dma((PANELS,)), dma((ROWS,)), dma((PANELS,)), dma((PANELS,)),
            dma((GROUP, 2)), dma((2,)),
        ],
        compiler_params=pltpu.CompilerParams(collective_id=0, has_side_effects=True),
        name="cascade",
    )(band_off, band_width, coupling, incident, cotangent)
    return sent.astype(f32)[None], back.astype(f32)[None]


def solution(mesh):
    in_specs = (P("layer", "row", None), P("layer"), P("layer"), P(None, "row"), P(None, "row"))
    out_specs = (P("layer", None, "row"), P("layer", None, "row"))
    return jax.shard_map(
        on_device, mesh=mesh, in_specs=in_specs, out_specs=out_specs, check_vma=False
    )
```

```python
import jax
import jax.numpy as jnp
from jax import lax
from jax.experimental import pallas as pl
from jax.experimental.pallas import tpu as pltpu
from jax.sharding import PartitionSpec as P

MESH = pl.DeviceIdType.MESH
BLOCK = 16
GROUP = 8
GROUPS = 8
ROWS = 8
PANELS = 4
ORDERS = 1024
TILE = 128
TILES = ORDERS // TILE
PANEL = ORDERS // PANELS
FIELDS = 32
LINE = 2 * GROUP
WIDEST = 3
WINDOW = 256
LEAD = 576
TRAIL = 640
PADDED = LEAD + ORDERS + TRAIL
SPAN = WINDOW // BLOCK
SENDS_AHEAD = 4
RELAYS_AHEAD = 2
DIRECT = (GROUP,)
FORWARD_Z = 7
f32 = jnp.float32
bf16 = jnp.bfloat16


def role_layer(group, kind):
    return LINE * (group // 2) + jnp.where(kind == 0, FORWARD_Z, 0)


def is_direct(i):
    found = i == DIRECT[0]
    for other in DIRECT[1:]:
        found = found | (i == other)
    return found


def kernel(off_ref, width_ref, coupling_ref, incident_ref, cotangent_ref, sent_ref, back_ref,
           scalars, local, mine, note, packs, notes, offsets, plain, flipped, banded, carry, high, low, even, odd,
           field_in, chain_in, chain_out, landed,
           load_sem, pack_send, pack_recv, note_send, note_recv, note_load, ring_send, ring_recv,
           field_send, field_recv, chain_send, chain_recv, spread_send, spread_recv):
    layer = lax.axis_index("layer")
    row = lax.axis_index("row")
    y = row // 2
    core = row % 2
    place_z = layer % LINE
    pair = layer // LINE
    own_group = layer // GROUP
    inner = layer % GROUP
    parity = own_group % 2
    targets = ((role_layer(own_group, 0), 2 * y + parity), (role_layer(own_group, 1), 2 * y + parity))
    is_target = [(layer == targets[w][0]) & (row == targets[w][1]) for w in range(2)]
    inside = is_target[0] | is_target[1]
    role = (place_z == 0) | (place_z == FORWARD_Z)
    kind = jnp.where(place_z == 0, 1, 0)
    group = 2 * pair + core
    place = jnp.where(kind == 0, group, GROUPS - 1 - group)
    first = place == 0
    final = place == GROUPS - 1
    ahead = jnp.where(kind == 0, jnp.minimum(group + 1, GROUPS - 1), jnp.maximum(group - 1, 0))
    behind = jnp.where(kind == 0, jnp.maximum(group - 1, 0), jnp.minimum(group + 1, GROUPS - 1))
    start_layers = (role_layer(0, 0), role_layer(GROUPS - 1, 1))
    at_start = (layer == start_layers[0]) | (layer == start_layers[1])
    start_core = jnp.where(layer == start_layers[0], 0, 1)
    up = (y + 1) % PANELS
    down = (y + PANELS - 1) % PANELS

    load = pltpu.make_async_copy(coupling_ref.at[0], local, load_sem.at[0])
    load.start()
    off_load = pltpu.make_async_copy(off_ref, scalars.at[0], load_sem.at[2])
    width_load = pltpu.make_async_copy(width_ref, scalars.at[1], load_sem.at[3])
    off_load.start()
    width_load.start()
    field_loads = [
        pltpu.make_async_copy(source, field_in.at[row], load_sem.at[1]) for source in (incident_ref, cotangent_ref)
    ]
    for which in range(2):
        @pl.when(layer == start_layers[which])
        def _(which=which):
            field_loads[which].start()

    barrier = pltpu.get_barrier_semaphore()

    def greet(to_layer, to_row):
        pl.semaphore_signal(barrier, inc=1, device_id={"layer": to_layer, "row": to_row}, device_id_type=MESH)

    for which in range(2):
        @pl.when(jnp.logical_not(is_target[which]))
        def _(which=which):
            greet(*targets[which])

    @pl.when(role)
    def _():
        for i in range(GROUP):
            for r in range(ROWS) if i in DIRECT else (2 * y, 2 * y + 1):
                @pl.when((GROUP * group + i != layer) | (r != row))
                def _(i=i, r=r):
                    greet(GROUP * group + i, r)
        greet(layer, 2 * up + core)
        greet(layer, 2 * down + core)

        @pl.when(jnp.logical_not(first))
        def _():
            for p in range(PANELS):
                greet(role_layer(behind, kind), 2 * p + behind % 2)

        @pl.when(first)
        def _():
            for step in range(1, ROWS):
                greet(layer, (row + step) % ROWS)

        for buffer in (high, low, even, odd):
            buffer[0:LEAD // BLOCK] = jnp.zeros((LEAD // BLOCK, BLOCK, PANEL), bf16)
            buffer[(LEAD + ORDERS) // BLOCK:PADDED // BLOCK] = jnp.zeros((TRAIL // BLOCK, BLOCK, PANEL), bf16)
        plain[0:LEAD // BLOCK] = jnp.zeros((LEAD // BLOCK, BLOCK, TILE), bf16)
        plain[(LEAD + ORDERS) // BLOCK:PADDED // BLOCK] = jnp.zeros((TRAIL // BLOCK, BLOCK, TILE), bf16)

    off_load.wait()
    width_load.wait()
    offset = scalars[0, 0]
    half_width = scalars[1, 0]
    note[...] = jnp.full((8, TILE), offset, jnp.int32)
    load.wait()
    here_row = lax.broadcasted_iota(jnp.int32, (TILE, TILE), 0) + TILE * row
    here_col = lax.broadcasted_iota(jnp.int32, (TILE, TILE), 1)
    folded = jnp.zeros((TILE, TILE), f32)
    for s in range(TILES):
        there = here_col + TILE * s
        apart = there // BLOCK - here_row // BLOCK
        upper = (there > here_row) & (jnp.abs(apart - offset) <= half_width)
        folded = folded + jnp.where(upper, local[:, TILE * s:TILE * s + TILE].astype(f32), 0.0)
    turn = jnp.broadcast_to(WIDEST + 40 - note[0:1, :], (TILE, TILE))
    for bit in range(3):
        folded = jnp.where((turn & (1 << bit)) != 0, pltpu.roll(folded, BLOCK << bit, 1), folded)
    mine[...] = folded.astype(bf16)

    @pl.when(inside)
    def _():
        packs[inner, row] = mine[...]

        @pl.when(core == 0)
        def _():
            notes[inner] = note[...]

    for which in range(2):
        @pl.when(layer == start_layers[which])
        def _(which=which):
            field_loads[which].wait()

    direct = is_direct(inner)
    def blocks_of(t):
        return slice((LEAD + TILE * t) // BLOCK, (LEAD + TILE * t + TILE) // BLOCK)

    def split(t, value):
        here = blocks_of(t)
        top = value.astype(bf16)
        high[here] = top.reshape(TILE // BLOCK, BLOCK, PANEL)
        low[here] = (value - top.astype(f32)).astype(bf16).reshape(TILE // BLOCK, BLOCK, PANEL)

    @pl.when(role & jnp.logical_not(first))
    def _():
        rows_at = lax.broadcasted_iota(jnp.int32, (ORDERS, PANEL), 0)
        cols_at = lax.broadcasted_iota(jnp.int32, (ORDERS, PANEL), 1)
        carry[...] = jnp.where(rows_at == cols_at + PANEL * y, 1.0, 0.0).astype(f32)
        for t in range(TILES):
            split(t, carry[TILE * t:TILE * t + TILE, :])

    expected = jnp.where(direct, 2 * PANELS, 2) - jnp.where(inside, 1, 0)
    expected = expected + jnp.where(role, 2 * GROUP + 2 - jnp.where(inside, 1, 0) + jnp.where(final, 0, PANELS), 0)
    expected = expected + jnp.where(at_start, PANELS - jnp.where(core == start_core, 1, 0), 0)
    pl.semaphore_wait(barrier, expected)

    def pack_copy(which, step):
        return pltpu.make_async_remote_copy(
            src_ref=mine, dst_ref=packs.at[inner, row],
            send_sem=pack_send.at[which, step], recv_sem=pack_recv.at[inner, row],
            device_id={"layer": targets[which][0], "row": 2 * ((y + step) % PANELS) + parity}, device_id_type=MESH)

    def note_copy(which):
        return pltpu.make_async_remote_copy(
            src_ref=note, dst_ref=notes.at[inner],
            send_sem=note_send.at[which], recv_sem=note_recv.at[inner],
            device_id={"layer": targets[which][0], "row": targets[which][1]}, device_id_type=MESH)

    for which in range(2):
        @pl.when(jnp.logical_not(is_target[which]))
        def _(which=which):
            pack_copy(which, 0).start()

            @pl.when(core == 0)
            def _():
                note_copy(which).start()

    @pl.when(direct)
    def _():
        for which in range(2):
            for step in range(1, PANELS):
                pack_copy(which, step).start()

    def field_copy(step):
        return pltpu.make_async_remote_copy(
            src_ref=field_in.at[row], dst_ref=field_in.at[row],
            send_sem=field_send.at[step], recv_sem=field_recv.at[row],
            device_id={"layer": layer, "row": 2 * ((y + step) % PANELS) + start_core}, device_id_type=MESH)

    @pl.when(at_start)
    def _():
        for step in range(PANELS):
            @pl.when((core != start_core) | (step != 0))
            def _(step=step):
                field_copy(step).start()

    def spread_copy(i, c):
        return pltpu.make_async_remote_copy(
            src_ref=chain_out.at[:, pl.ds(TILE * c, TILE)], dst_ref=landed.at[kind],
            send_sem=spread_send.at[i, c], recv_sem=spread_recv.at[kind],
            device_id={"layer": GROUP * group + i, "row": 2 * y + c}, device_id_type=MESH)

    @pl.when(role)
    def _():
        forward_order = (kind == 1) != first
        sign = jnp.where(forward_order, 1.0, -1.0).astype(f32)

        def nth(k):
            return jnp.where(forward_order, k, GROUP - 1 - k)

        def local_pack(i, c):
            return (GROUP * group + i == layer) & (c == core)

        def wait_pack(i, r):
            @pl.when((GROUP * group + i != layer) | (r != row))
            def _():
                pltpu.make_async_remote_copy(
                    src_ref=mine, dst_ref=packs.at[i, r],
                    send_sem=pack_send.at[0, 0], recv_sem=pack_recv.at[i, r],
                    device_id={"layer": layer, "row": 2 * up + core}, device_id_type=MESH).wait_recv()

        def pair_copy(i, toward, slot):
            return pltpu.make_async_remote_copy(
                src_ref=packs.at[i, pl.ds(2 * y, 2)], dst_ref=packs.at[i, pl.ds(2 * y, 2)],
                send_sem=ring_send.at[i, slot], recv_sem=ring_recv.at[i, slot],
                device_id={"layer": layer, "row": 2 * toward + core}, device_id_type=MESH)

        def pair_wait(i, source, slot):
            pltpu.make_async_remote_copy(
                src_ref=packs.at[i, pl.ds(2 * source, 2)], dst_ref=packs.at[i, pl.ds(2 * source, 2)],
                send_sem=ring_send.at[i, slot], recv_sem=ring_recv.at[i, slot],
                device_id={"layer": layer, "row": 2 * source + core}, device_id_type=MESH).wait_recv()

        def half_copy(i, r, toward, slot):
            return pltpu.make_async_remote_copy(
                src_ref=packs.at[i, r], dst_ref=packs.at[i, r],
                send_sem=ring_send.at[i, slot], recv_sem=ring_recv.at[i, slot],
                device_id={"layer": layer, "row": 2 * toward + core}, device_id_type=MESH)

        across = (y + 2) % PANELS

        def send_round(k):
            i = nth(k)

            @pl.when(jnp.logical_not(is_direct(i)))
            def _():
                wait_pack(i, 2 * y)
                wait_pack(i, 2 * y + 1)
                pair_copy(i, up, 0).start()
                pair_copy(i, down, 1).start()

        def relay_round(k):
            i = nth(k)

            @pl.when(jnp.logical_not(is_direct(i)))
            def _():
                pair_wait(i, down, 0)
                half_copy(i, 2 * down, up, 2).start()
                pair_wait(i, up, 1)
                half_copy(i, 2 * up + 1, down, 3).start()

        def finish_round(k):
            i = nth(k)

            @pl.when(jnp.logical_not(is_direct(i)))
            def _():
                half_copy(i, 2 * across, up, 2).wait_recv()
                half_copy(i, 2 * across + 1, down, 3).wait_recv()

            @pl.when(is_direct(i))
            def _():
                for r in range(ROWS):
                    wait_pack(i, r)

        def note_fetch(i):
            return pltpu.make_async_copy(notes.at[i], offsets.at[i], note_load.at[i])

        def note_round(k):
            i = nth(k)

            @pl.when(jnp.logical_not(local_pack(i, 0)))
            def _():
                pltpu.make_async_remote_copy(
                    src_ref=note, dst_ref=notes.at[i],
                    send_sem=note_send.at[0], recv_sem=note_recv.at[i],
                    device_id={"layer": layer, "row": 2 * up + core}, device_id_type=MESH).wait_recv()
            note_fetch(i).start()

        for k in range(SENDS_AHEAD):
            send_round(k)
        note_round(0)
        for k in range(RELAYS_AHEAD):
            relay_round(k)

        @pl.when(first)
        def _():
            for r in range(ROWS):
                @pl.when(r != row)
                def _(r=r):
                    pltpu.make_async_remote_copy(
                        src_ref=field_in.at[r], dst_ref=field_in.at[r],
                        send_sem=field_send.at[0], recv_sem=field_recv.at[r],
                        device_id={"layer": layer, "row": (row + 1) % ROWS}, device_id_type=MESH).wait_recv()
                tall = jnp.concatenate([field_in[r], jnp.zeros((TILE - FIELDS, TILE), f32)], axis=0)
                carry[TILE * r:TILE * r + TILE, 0:TILE] = tall.T
            carry[:, TILE:PANEL] = jnp.zeros((ORDERS, PANEL - TILE), f32)
            for t in range(TILES):
                split(t, carry[TILE * t:TILE * t + TILE, :])

        slot = lax.broadcasted_iota(jnp.int32, (TILE, WINDOW), 1) // BLOCK
        step = lax.broadcasted_iota(jnp.int32, (TILE, WINDOW), 0) // BLOCK
        near = jnp.abs(slot - step - WIDEST) <= WIDEST
        upper_mask = jnp.where(near, sign, 0.0).astype(bf16)
        lower_mask = jnp.where(near, -sign, 0.0).astype(bf16)

        @pl.loop(0, GROUP)
        def _(k):
            @pl.when(k + SENDS_AHEAD < GROUP)
            def _():
                send_round(k + SENDS_AHEAD)

            @pl.when(k + RELAYS_AHEAD < GROUP)
            def _():
                relay_round(k + RELAYS_AHEAD)

            @pl.when(k + 1 < GROUP)
            def _():
                note_round(k + 1)
            i = nth(k)
            finish_round(k)
            note_fetch(i).wait()
            off = offsets[i, 0, 0]
            turn = (WIDEST + 40 - off) % 8

            def upper_at(t):
                return pl.ds((LEAD + TILE * t) // BLOCK - WIDEST + off, SPAN)

            def lower_at(t):
                return pl.ds((LEAD + TILE * t) // BLOCK - WIDEST - off, SPAN)

            for t in range(TILES):
                value = packs[i, t]
                plain[blocks_of(t)] = value.reshape(TILE // BLOCK, BLOCK, TILE)
                banded[t, :, 0:WINDOW] = jnp.concatenate([value, value], axis=1) * upper_mask
            for t in range(TILES):
                tall = plain[lower_at(t)].reshape(WINDOW, TILE).T.reshape(TILE // BLOCK, BLOCK, WINDOW)
                flipped[t, 0:TILE // BLOCK] = tall
                flipped[t, TILE // BLOCK:2 * TILE // BLOCK] = tall
            for t in range(TILES):
                tall = flipped[t, pl.ds(turn, TILE // BLOCK)].reshape(TILE, WINDOW)
                banded[t, :, WINDOW:2 * WINDOW] = tall * lower_mask

            def product(t, source):
                both = jnp.concatenate([source[upper_at(t)].reshape(WINDOW, PANEL),
                                        source[lower_at(t)].reshape(WINDOW, PANEL)], axis=0)
                return jnp.dot(banded[t], both, preferred_element_type=f32)

            for order, source, target in ((1, high, even), (2, even, odd), (3, odd, even), (4, even, None)):
                for t in range(TILES):
                    here = slice(TILE * t, TILE * t + TILE)
                    term = product(t, source)
                    if order == 1:
                        term = term + product(t, low)
                    else:
                        term = term * (1.0 / order)
                    total = carry[here, :] + term
                    carry[here, :] = total
                    if target is None:
                        split(t, total)
                    else:
                        target[blocks_of(t)] = term.astype(bf16).reshape(TILE // BLOCK, BLOCK, PANEL)

        @pl.when(first)
        def _():
            part = carry[pl.ds(pl.multiple_of(PANEL * y, PANEL), PANEL), 0:TILE]
            chain_out[...] = part.T[0:FIELDS, :].astype(bf16)

        @pl.when(jnp.logical_not(first))
        def _():
            summed = jnp.zeros((FIELDS, PANEL), f32)
            for p in range(PANELS):
                pltpu.make_async_remote_copy(
                    src_ref=chain_out, dst_ref=chain_in.at[p],
                    send_sem=chain_send.at[0], recv_sem=chain_recv.at[p],
                    device_id={"layer": layer, "row": 2 * up + core}, device_id_type=MESH).wait_recv()
                summed = summed + jnp.dot(chain_in[p], high[(LEAD + PANEL * p) // BLOCK:(LEAD + PANEL * p + PANEL) // BLOCK].reshape(PANEL, PANEL),
                                          preferred_element_type=f32)
            chain_out[...] = summed.astype(bf16)

        def chain_copy(p):
            return pltpu.make_async_remote_copy(
                src_ref=chain_out, dst_ref=chain_in.at[y],
                send_sem=chain_send.at[p], recv_sem=chain_recv.at[y],
                device_id={"layer": role_layer(ahead, kind), "row": 2 * p + ahead % 2}, device_id_type=MESH)

        @pl.when(jnp.logical_not(final))
        def _():
            for p in range(PANELS):
                chain_copy(p).start()

        for i in range(GROUP):
            for c in range(2):
                @pl.when(jnp.logical_not(local_pack(i, c)))
                def _(i=i, c=c):
                    spread_copy(i, c).start()

        @pl.when(inside)
        def _():
            landed[kind] = jnp.where(core == 0, chain_out[:, 0:TILE], chain_out[:, TILE:PANEL])

        for i in [j for j in range(GROUP) if j not in DIRECT]:
            pair_copy(i, up, 0).wait_send()
            pair_copy(i, down, 1).wait_send()
            half_copy(i, 2 * down, up, 2).wait_send()
            half_copy(i, 2 * up + 1, down, 3).wait_send()

        @pl.when(jnp.logical_not(final))
        def _():
            for p in range(PANELS):
                chain_copy(p).wait_send()
        for i in range(GROUP):
            for c in range(2):
                @pl.when(jnp.logical_not(local_pack(i, c)))
                def _(i=i, c=c):
                    spread_copy(i, c).wait_send()

    for which in range(2):
        @pl.when(jnp.logical_not(is_target[which]))
        def _(which=which):
            pack_copy(which, 0).wait_send()

            @pl.when(core == 0)
            def _():
                note_copy(which).wait_send()

    @pl.when(direct)
    def _():
        for which in range(2):
            for step in range(1, PANELS):
                pack_copy(which, step).wait_send()

    @pl.when(at_start)
    def _():
        for step in range(PANELS):
            @pl.when((core != start_core) | (step != 0))
            def _(step=step):
                field_copy(step).wait_send()

    for which, out in ((0, sent_ref), (1, back_ref)):
        @pl.when(jnp.logical_not(is_target[which]))
        def _(which=which):
            pltpu.make_async_remote_copy(
                src_ref=chain_out.at[:, pl.ds(0, TILE)], dst_ref=landed.at[which],
                send_sem=spread_send.at[0, 0], recv_sem=spread_recv.at[which],
                device_id={"layer": targets[which][0], "row": targets[which][1]}, device_id_type=MESH).wait_recv()
        out[...] = landed[which]


def on_device(coupling, band_off, band_width, incident, cotangent):
    vmem = pl.BlockSpec(memory_space=pltpu.VMEM)
    away = pl.BlockSpec(memory_space=pl.ANY)
    dma = pltpu.SemaphoreType.DMA
    share = jax.ShapeDtypeStruct((FIELDS, TILE), bf16)
    sent, back = pl.pallas_call(
        kernel,
        out_shape=(share, share),
        in_specs=[away] * 5,
        out_specs=(vmem, vmem),
        scratch_shapes=[
            pltpu.SMEM((2, 1), jnp.int32),
            pltpu.VMEM((TILE, ORDERS), bf16),
            pltpu.VMEM((TILE, TILE), bf16),
            pltpu.VMEM((8, TILE), jnp.int32),
            pltpu.VMEM((GROUP, ROWS, TILE, TILE), bf16),
            pltpu.VMEM((GROUP, 8, TILE), jnp.int32),
            pltpu.SMEM((GROUP, 8, TILE), jnp.int32),
            pltpu.VMEM((PADDED // BLOCK, BLOCK, TILE), bf16),
            pltpu.VMEM((TILES, 2 * TILE // BLOCK, BLOCK, WINDOW), bf16),
            pltpu.VMEM((TILES, TILE, 2 * WINDOW), bf16),
            pltpu.VMEM((ORDERS, PANEL), f32),
            pltpu.VMEM((PADDED // BLOCK, BLOCK, PANEL), bf16),
            pltpu.VMEM((PADDED // BLOCK, BLOCK, PANEL), bf16),
            pltpu.VMEM((PADDED // BLOCK, BLOCK, PANEL), bf16),
            pltpu.VMEM((PADDED // BLOCK, BLOCK, PANEL), bf16),
            pltpu.VMEM((ROWS, FIELDS, TILE), f32),
            pltpu.VMEM((PANELS, FIELDS, PANEL), bf16),
            pltpu.VMEM((FIELDS, PANEL), bf16),
            pltpu.VMEM((2, FIELDS, TILE), bf16),
            dma((4,)), dma((2, PANELS)), dma((GROUP, ROWS)), dma((2,)), dma((GROUP,)), dma((GROUP,)),
            dma((GROUP, 4)), dma((GROUP, 4)), dma((PANELS,)), dma((ROWS,)), dma((PANELS,)), dma((PANELS,)),
            dma((GROUP, 2)), dma((2,)),
        ],
        compiler_params=pltpu.CompilerParams(collective_id=0, has_side_effects=True),
        name="cascade",
    )(band_off, band_width, coupling, incident, cotangent)
    return sent.astype(f32)[None], back.astype(f32)[None]


def solution(mesh):
    in_specs = (P("layer", "row", None), P("layer"), P("layer"), P(None, "row"), P(None, "row"))
    out_specs = (P("layer", None, "row"), P("layer", None, "row"))
    return jax.shard_map(
        on_device, mesh=mesh, in_specs=in_specs, out_specs=out_specs, check_vma=False
    )
```

```python
import jax
import jax.numpy as jnp
from jax import lax
from jax.experimental import pallas as pl
from jax.experimental.pallas import tpu as pltpu
from jax.sharding import PartitionSpec as P

MESH = pl.DeviceIdType.MESH
BLOCK = 16
GROUP = 8
GROUPS = 8
ROWS = 8
PANELS = 4
ORDERS = 1024
TILE = 128
TILES = ORDERS // TILE
PANEL = ORDERS // PANELS
FIELDS = 32
LINE = 2 * GROUP
WIDEST = 3
WINDOW = 256
LEAD = 576
TRAIL = 640
PADDED = LEAD + ORDERS + TRAIL
SPAN = WINDOW // BLOCK
SENDS_AHEAD = 4
RELAYS_AHEAD = 2
DIRECT = (GROUP,)
FORWARD_Z = 7
f32 = jnp.float32
bf16 = jnp.bfloat16


def role_layer(group, kind):
    return LINE * (group // 2) + jnp.where(kind == 0, FORWARD_Z, 0)


def is_direct(i):
    found = i == DIRECT[0]
    for other in DIRECT[1:]:
        found = found | (i == other)
    return found


def kernel(off_ref, width_ref, coupling_ref, incident_ref, cotangent_ref, sent_ref, back_ref,
           scalars, local, mine, note, packs, notes, offsets, plain, flipped, banded, carry, high, low, even, odd,
           field_in, chain_in, chain_out, landed,
           load_sem, pack_send, pack_recv, note_send, note_recv, note_load, ring_send, ring_recv,
           field_send, field_recv, chain_send, chain_recv, spread_send, spread_recv):
    layer = lax.axis_index("layer")
    row = lax.axis_index("row")
    y = row // 2
    core = row % 2
    place_z = layer % LINE
    pair = layer // LINE
    own_group = layer // GROUP
    inner = layer % GROUP
    parity = own_group % 2
    targets = ((role_layer(own_group, 0), 2 * y + parity), (role_layer(own_group, 1), 2 * y + parity))
    is_target = [(layer == targets[w][0]) & (row == targets[w][1]) for w in range(2)]
    inside = is_target[0] | is_target[1]
    role = (place_z == 0) | (place_z == FORWARD_Z)
    kind = jnp.where(place_z == 0, 1, 0)
    group = 2 * pair + core
    place = jnp.where(kind == 0, group, GROUPS - 1 - group)
    first = place == 0
    final = place == GROUPS - 1
    ahead = jnp.where(kind == 0, jnp.minimum(group + 1, GROUPS - 1), jnp.maximum(group - 1, 0))
    behind = jnp.where(kind == 0, jnp.maximum(group - 1, 0), jnp.minimum(group + 1, GROUPS - 1))
    start_layers = (role_layer(0, 0), role_layer(GROUPS - 1, 1))
    at_start = (layer == start_layers[0]) | (layer == start_layers[1])
    start_core = jnp.where(layer == start_layers[0], 0, 1)
    up = (y + 1) % PANELS
    down = (y + PANELS - 1) % PANELS

    load = pltpu.make_async_copy(coupling_ref.at[0], local, load_sem.at[0])
    load.start()
    off_load = pltpu.make_async_copy(off_ref, scalars.at[0], load_sem.at[2])
    width_load = pltpu.make_async_copy(width_ref, scalars.at[1], load_sem.at[3])
    off_load.start()
    width_load.start()
    field_loads = [
        pltpu.make_async_copy(source, field_in.at[row], load_sem.at[1]) for source in (incident_ref, cotangent_ref)
    ]
    for which in range(2):
        @pl.when(layer == start_layers[which])
        def _(which=which):
            field_loads[which].start()

    barrier = pltpu.get_barrier_semaphore()

    def greet(to_layer, to_row):
        pl.semaphore_signal(barrier, inc=1, device_id={"layer": to_layer, "row": to_row}, device_id_type=MESH)

    for which in range(2):
        @pl.when(jnp.logical_not(is_target[which]))
        def _(which=which):
            greet(*targets[which])

    @pl.when(role)
    def _():
        for i in range(GROUP):
            for r in range(ROWS) if i in DIRECT else (2 * y, 2 * y + 1):
                @pl.when((GROUP * group + i != layer) | (r != row))
                def _(i=i, r=r):
                    greet(GROUP * group + i, r)
        greet(layer, 2 * up + core)
        greet(layer, 2 * down + core)

        @pl.when(jnp.logical_not(first))
        def _():
            for p in range(PANELS):
                greet(role_layer(behind, kind), 2 * p + behind % 2)

        @pl.when(first)
        def _():
            for step in range(1, ROWS):
                greet(layer, (row + step) % ROWS)

        for buffer in (high, low, even, odd):
            buffer[0:LEAD // BLOCK] = jnp.zeros((LEAD // BLOCK, BLOCK, PANEL), bf16)
            buffer[(LEAD + ORDERS) // BLOCK:PADDED // BLOCK] = jnp.zeros((TRAIL // BLOCK, BLOCK, PANEL), bf16)
        plain[0:LEAD // BLOCK] = jnp.zeros((LEAD // BLOCK, BLOCK, TILE), bf16)
        plain[(LEAD + ORDERS) // BLOCK:PADDED // BLOCK] = jnp.zeros((TRAIL // BLOCK, BLOCK, TILE), bf16)

    off_load.wait()
    width_load.wait()
    offset = scalars[0, 0]
    half_width = scalars[1, 0]
    note[...] = jnp.full((8, TILE), offset, jnp.int32)
    load.wait()
    here_row = lax.broadcasted_iota(jnp.int32, (TILE, TILE), 0) + TILE * row
    here_col = lax.broadcasted_iota(jnp.int32, (TILE, TILE), 1)
    folded = jnp.zeros((TILE, TILE), f32)
    for s in range(TILES):
        there = here_col + TILE * s
        apart = there // BLOCK - here_row // BLOCK
        upper = (there > here_row) & (jnp.abs(apart - offset) <= half_width)
        folded = folded + jnp.where(upper, local[:, TILE * s:TILE * s + TILE].astype(f32), 0.0)
    turn = jnp.broadcast_to(WIDEST + 40 - note[0:1, :], (TILE, TILE))
    for bit in range(3):
        folded = jnp.where((turn & (1 << bit)) != 0, pltpu.roll(folded, BLOCK << bit, 1), folded)
    mine[...] = folded.astype(bf16)

    @pl.when(inside)
    def _():
        packs[inner, row] = mine[...]

        @pl.when(core == 0)
        def _():
            notes[inner] = note[...]

    for which in range(2):
        @pl.when(layer == start_layers[which])
        def _(which=which):
            field_loads[which].wait()

    direct = is_direct(inner)
    def blocks_of(t):
        return slice((LEAD + TILE * t) // BLOCK, (LEAD + TILE * t + TILE) // BLOCK)

    def split(t, value):
        here = blocks_of(t)
        top = value.astype(bf16)
        high[here] = top.reshape(TILE // BLOCK, BLOCK, PANEL)
        low[here] = (value - top.astype(f32)).astype(bf16).reshape(TILE // BLOCK, BLOCK, PANEL)

    @pl.when(role & jnp.logical_not(first))
    def _():
        rows_at = lax.broadcasted_iota(jnp.int32, (ORDERS, PANEL), 0)
        cols_at = lax.broadcasted_iota(jnp.int32, (ORDERS, PANEL), 1)
        carry[...] = jnp.where(rows_at == cols_at + PANEL * y, 1.0, 0.0).astype(f32)
        for t in range(TILES):
            split(t, carry[TILE * t:TILE * t + TILE, :])

    expected = jnp.where(direct, 2 * PANELS, 2) - jnp.where(inside, 1, 0)
    expected = expected + jnp.where(role, 2 * GROUP + 2 - jnp.where(inside, 1, 0) + jnp.where(final, 0, PANELS), 0)
    expected = expected + jnp.where(at_start, PANELS - jnp.where(core == start_core, 1, 0), 0)
    pl.semaphore_wait(barrier, expected)

    def pack_copy(which, step):
        return pltpu.make_async_remote_copy(
            src_ref=mine, dst_ref=packs.at[inner, row],
            send_sem=pack_send.at[which, step], recv_sem=pack_recv.at[inner, row],
            device_id={"layer": targets[which][0], "row": 2 * ((y + step) % PANELS) + parity}, device_id_type=MESH)

    def note_copy(which):
        return pltpu.make_async_remote_copy(
            src_ref=note, dst_ref=notes.at[inner],
            send_sem=note_send.at[which], recv_sem=note_recv.at[inner],
            device_id={"layer": targets[which][0], "row": targets[which][1]}, device_id_type=MESH)

    for which in range(2):
        @pl.when(jnp.logical_not(is_target[which]))
        def _(which=which):
            pack_copy(which, 0).start()

            @pl.when(core == 0)
            def _():
                note_copy(which).start()

    @pl.when(direct)
    def _():
        for which in range(2):
            for step in range(1, PANELS):
                pack_copy(which, step).start()

    def field_copy(step):
        return pltpu.make_async_remote_copy(
            src_ref=field_in.at[row], dst_ref=field_in.at[row],
            send_sem=field_send.at[step], recv_sem=field_recv.at[row],
            device_id={"layer": layer, "row": 2 * ((y + step) % PANELS) + start_core}, device_id_type=MESH)

    @pl.when(at_start)
    def _():
        for step in range(PANELS):
            @pl.when((core != start_core) | (step != 0))
            def _(step=step):
                field_copy(step).start()

    def spread_copy(i, c):
        return pltpu.make_async_remote_copy(
            src_ref=chain_out.at[:, pl.ds(TILE * c, TILE)], dst_ref=landed.at[kind],
            send_sem=spread_send.at[i, c], recv_sem=spread_recv.at[kind],
            device_id={"layer": GROUP * group + i, "row": 2 * y + c}, device_id_type=MESH)

    @pl.when(role)
    def _():
        forward_order = (kind == 1) != first
        sign = jnp.where(forward_order, 1.0, -1.0).astype(f32)

        def nth(k):
            return jnp.where(forward_order, k, GROUP - 1 - k)

        def local_pack(i, c):
            return (GROUP * group + i == layer) & (c == core)

        def wait_pack(i, r):
            @pl.when((GROUP * group + i != layer) | (r != row))
            def _():
                pltpu.make_async_remote_copy(
                    src_ref=mine, dst_ref=packs.at[i, r],
                    send_sem=pack_send.at[0, 0], recv_sem=pack_recv.at[i, r],
                    device_id={"layer": layer, "row": 2 * up + core}, device_id_type=MESH).wait_recv()

        def pair_copy(i, toward, slot):
            return pltpu.make_async_remote_copy(
                src_ref=packs.at[i, pl.ds(2 * y, 2)], dst_ref=packs.at[i, pl.ds(2 * y, 2)],
                send_sem=ring_send.at[i, slot], recv_sem=ring_recv.at[i, slot],
                device_id={"layer": layer, "row": 2 * toward + core}, device_id_type=MESH)

        def pair_wait(i, source, slot):
            pltpu.make_async_remote_copy(
                src_ref=packs.at[i, pl.ds(2 * source, 2)], dst_ref=packs.at[i, pl.ds(2 * source, 2)],
                send_sem=ring_send.at[i, slot], recv_sem=ring_recv.at[i, slot],
                device_id={"layer": layer, "row": 2 * source + core}, device_id_type=MESH).wait_recv()

        def half_copy(i, r, toward, slot):
            return pltpu.make_async_remote_copy(
                src_ref=packs.at[i, r], dst_ref=packs.at[i, r],
                send_sem=ring_send.at[i, slot], recv_sem=ring_recv.at[i, slot],
                device_id={"layer": layer, "row": 2 * toward + core}, device_id_type=MESH)

        across = (y + 2) % PANELS

        def send_round(k):
            i = nth(k)

            @pl.when(jnp.logical_not(is_direct(i)))
            def _():
                wait_pack(i, 2 * y)
                wait_pack(i, 2 * y + 1)
                pair_copy(i, up, 0).start()
                pair_copy(i, down, 1).start()

        def relay_round(k):
            i = nth(k)

            @pl.when(jnp.logical_not(is_direct(i)))
            def _():
                pair_wait(i, down, 0)
                half_copy(i, 2 * down, up, 2).start()
                pair_wait(i, up, 1)
                half_copy(i, 2 * up + 1, down, 3).start()

        def finish_round(k):
            i = nth(k)

            @pl.when(jnp.logical_not(is_direct(i)))
            def _():
                half_copy(i, 2 * across, up, 2).wait_recv()
                half_copy(i, 2 * across + 1, down, 3).wait_recv()

            @pl.when(is_direct(i))
            def _():
                for r in range(ROWS):
                    wait_pack(i, r)

        def note_fetch(i):
            return pltpu.make_async_copy(notes.at[i], offsets.at[i], note_load.at[i])

        def note_round(k):
            i = nth(k)

            @pl.when(jnp.logical_not(local_pack(i, 0)))
            def _():
                pltpu.make_async_remote_copy(
                    src_ref=note, dst_ref=notes.at[i],
                    send_sem=note_send.at[0], recv_sem=note_recv.at[i],
                    device_id={"layer": layer, "row": 2 * up + core}, device_id_type=MESH).wait_recv()
            note_fetch(i).start()

        for k in range(SENDS_AHEAD):
            send_round(k)
        note_round(0)
        for k in range(RELAYS_AHEAD):
            relay_round(k)

        @pl.when(first)
        def _():
            for r in range(ROWS):
                @pl.when(r != row)
                def _(r=r):
                    pltpu.make_async_remote_copy(
                        src_ref=field_in.at[r], dst_ref=field_in.at[r],
                        send_sem=field_send.at[0], recv_sem=field_recv.at[r],
                        device_id={"layer": layer, "row": (row + 1) % ROWS}, device_id_type=MESH).wait_recv()
                tall = jnp.concatenate([field_in[r], jnp.zeros((TILE - FIELDS, TILE), f32)], axis=0)
                carry[TILE * r:TILE * r + TILE, 0:TILE] = tall.T
            carry[:, TILE:PANEL] = jnp.zeros((ORDERS, PANEL - TILE), f32)
            for t in range(TILES):
                split(t, carry[TILE * t:TILE * t + TILE, :])

        slot = lax.broadcasted_iota(jnp.int32, (TILE, WINDOW), 1) // BLOCK
        step = lax.broadcasted_iota(jnp.int32, (TILE, WINDOW), 0) // BLOCK
        near = jnp.abs(slot - step - WIDEST) <= WIDEST
        upper_mask = jnp.where(near, sign, 0.0).astype(bf16)
        lower_mask = jnp.where(near, -sign, 0.0).astype(bf16)

        @pl.loop(0, GROUP)
        def _(k):
            @pl.when(k + SENDS_AHEAD < GROUP)
            def _():
                send_round(k + SENDS_AHEAD)

            @pl.when(k + RELAYS_AHEAD < GROUP)
            def _():
                relay_round(k + RELAYS_AHEAD)

            @pl.when(k + 1 < GROUP)
            def _():
                note_round(k + 1)
            i = nth(k)
            finish_round(k)
            note_fetch(i).wait()
            off = offsets[i, 0, 0]
            turn = (WIDEST + 40 - off) % 8

            def upper_at(t):
                return pl.ds((LEAD + TILE * t) // BLOCK - WIDEST + off, SPAN)

            def lower_at(t):
                return pl.ds((LEAD + TILE * t) // BLOCK - WIDEST - off, SPAN)

            for t in range(TILES):
                value = packs[i, t]
                plain[blocks_of(t)] = value.reshape(TILE // BLOCK, BLOCK, TILE)
                banded[t, :, 0:WINDOW] = jnp.concatenate([value, value], axis=1) * upper_mask
            for t in range(TILES):
                tall = plain[lower_at(t)].reshape(WINDOW, TILE).T.reshape(TILE // BLOCK, BLOCK, WINDOW)
                flipped[t, 0:TILE // BLOCK] = tall
                flipped[t, TILE // BLOCK:2 * TILE // BLOCK] = tall
            for t in range(TILES):
                tall = flipped[t, pl.ds(turn, TILE // BLOCK)].reshape(TILE, WINDOW)
                banded[t, :, WINDOW:2 * WINDOW] = tall * lower_mask

            def product(t, source):
                both = jnp.concatenate([source[upper_at(t)].reshape(WINDOW, PANEL),
                                        source[lower_at(t)].reshape(WINDOW, PANEL)], axis=0)
                return jnp.dot(banded[t], both, preferred_element_type=f32)

            for order, source, target in ((1, high, even), (2, even, odd), (3, odd, even), (4, even, None)):
                for t in range(TILES):
                    here = slice(TILE * t, TILE * t + TILE)
                    term = product(t, source)
                    if order == 1:
                        term = term + product(t, low)
                    else:
                        term = term * (1.0 / order)
                    total = carry[here, :] + term
                    carry[here, :] = total
                    if target is None:
                        split(t, total)
                    else:
                        target[blocks_of(t)] = term.astype(bf16).reshape(TILE // BLOCK, BLOCK, PANEL)

        @pl.when(first)
        def _():
            part = carry[pl.ds(pl.multiple_of(PANEL * y, PANEL), PANEL), 0:TILE]
            chain_out[...] = part.T[0:FIELDS, :].astype(bf16)

        @pl.when(jnp.logical_not(first))
        def _():
            summed = jnp.zeros((FIELDS, PANEL), f32)
            for p in range(PANELS):
                pltpu.make_async_remote_copy(
                    src_ref=chain_out, dst_ref=chain_in.at[p],
                    send_sem=chain_send.at[0], recv_sem=chain_recv.at[p],
                    device_id={"layer": layer, "row": 2 * up + core}, device_id_type=MESH).wait_recv()
                summed = summed + jnp.dot(chain_in[p], high[(LEAD + PANEL * p) // BLOCK:(LEAD + PANEL * p + PANEL) // BLOCK].reshape(PANEL, PANEL),
                                          preferred_element_type=f32)
            chain_out[...] = summed.astype(bf16)

        def chain_copy(p):
            return pltpu.make_async_remote_copy(
                src_ref=chain_out, dst_ref=chain_in.at[y],
                send_sem=chain_send.at[p], recv_sem=chain_recv.at[y],
                device_id={"layer": role_layer(ahead, kind), "row": 2 * p + ahead % 2}, device_id_type=MESH)

        @pl.when(jnp.logical_not(final))
        def _():
            for p in range(PANELS):
                chain_copy(p).start()

        for i in reversed(range(GROUP)):
            for c in range(2):
                @pl.when(jnp.logical_not(local_pack(i, c)))
                def _(i=i, c=c):
                    spread_copy(i, c).start()

        @pl.when(inside)
        def _():
            landed[kind] = jnp.where(core == 0, chain_out[:, 0:TILE], chain_out[:, TILE:PANEL])

        for i in [j for j in range(GROUP) if j not in DIRECT]:
            pair_copy(i, up, 0).wait_send()
            pair_copy(i, down, 1).wait_send()
            half_copy(i, 2 * down, up, 2).wait_send()
            half_copy(i, 2 * up + 1, down, 3).wait_send()

        @pl.when(jnp.logical_not(final))
        def _():
            for p in range(PANELS):
                chain_copy(p).wait_send()
        for i in range(GROUP):
            for c in range(2):
                @pl.when(jnp.logical_not(local_pack(i, c)))
                def _(i=i, c=c):
                    spread_copy(i, c).wait_send()

    for which in range(2):
        @pl.when(jnp.logical_not(is_target[which]))
        def _(which=which):
            pack_copy(which, 0).wait_send()

            @pl.when(core == 0)
            def _():
                note_copy(which).wait_send()

    @pl.when(direct)
    def _():
        for which in range(2):
            for step in range(1, PANELS):
                pack_copy(which, step).wait_send()

    @pl.when(at_start)
    def _():
        for step in range(PANELS):
            @pl.when((core != start_core) | (step != 0))
            def _(step=step):
                field_copy(step).wait_send()

    for which, out in ((0, sent_ref), (1, back_ref)):
        @pl.when(jnp.logical_not(is_target[which]))
        def _(which=which):
            pltpu.make_async_remote_copy(
                src_ref=chain_out.at[:, pl.ds(0, TILE)], dst_ref=landed.at[which],
                send_sem=spread_send.at[0, 0], recv_sem=spread_recv.at[which],
                device_id={"layer": targets[which][0], "row": targets[which][1]}, device_id_type=MESH).wait_recv()
        out[...] = landed[which]


def on_device(coupling, band_off, band_width, incident, cotangent):
    vmem = pl.BlockSpec(memory_space=pltpu.VMEM)
    away = pl.BlockSpec(memory_space=pl.ANY)
    dma = pltpu.SemaphoreType.DMA
    share = jax.ShapeDtypeStruct((FIELDS, TILE), bf16)
    sent, back = pl.pallas_call(
        kernel,
        out_shape=(share, share),
        in_specs=[away] * 5,
        out_specs=(vmem, vmem),
        scratch_shapes=[
            pltpu.SMEM((2, 1), jnp.int32),
            pltpu.VMEM((TILE, ORDERS), bf16),
            pltpu.VMEM((TILE, TILE), bf16),
            pltpu.VMEM((8, TILE), jnp.int32),
            pltpu.VMEM((GROUP, ROWS, TILE, TILE), bf16),
            pltpu.VMEM((GROUP, 8, TILE), jnp.int32),
            pltpu.SMEM((GROUP, 8, TILE), jnp.int32),
            pltpu.VMEM((PADDED // BLOCK, BLOCK, TILE), bf16),
            pltpu.VMEM((TILES, 2 * TILE // BLOCK, BLOCK, WINDOW), bf16),
            pltpu.VMEM((TILES, TILE, 2 * WINDOW), bf16),
            pltpu.VMEM((ORDERS, PANEL), f32),
            pltpu.VMEM((PADDED // BLOCK, BLOCK, PANEL), bf16),
            pltpu.VMEM((PADDED // BLOCK, BLOCK, PANEL), bf16),
            pltpu.VMEM((PADDED // BLOCK, BLOCK, PANEL), bf16),
            pltpu.VMEM((PADDED // BLOCK, BLOCK, PANEL), bf16),
            pltpu.VMEM((ROWS, FIELDS, TILE), f32),
            pltpu.VMEM((PANELS, FIELDS, PANEL), bf16),
            pltpu.VMEM((FIELDS, PANEL), bf16),
            pltpu.VMEM((2, FIELDS, TILE), bf16),
            dma((4,)), dma((2, PANELS)), dma((GROUP, ROWS)), dma((2,)), dma((GROUP,)), dma((GROUP,)),
            dma((GROUP, 4)), dma((GROUP, 4)), dma((PANELS,)), dma((ROWS,)), dma((PANELS,)), dma((PANELS,)),
            dma((GROUP, 2)), dma((2,)),
        ],
        compiler_params=pltpu.CompilerParams(collective_id=0, has_side_effects=True),
        name="cascade",
    )(band_off, band_width, coupling, incident, cotangent)
    return sent.astype(f32)[None], back.astype(f32)[None]


def solution(mesh):
    in_specs = (P("layer", "row", None), P("layer"), P("layer"), P(None, "row"), P(None, "row"))
    out_specs = (P("layer", None, "row"), P("layer", None, "row"))
    return jax.shard_map(
        on_device, mesh=mesh, in_specs=in_specs, out_specs=out_specs, check_vma=False
    )
```
